32 devices in a mesh: vol: 8 (over y, x, core), surf: 4 (over z).
Axes of the slice: x: 2, y: 2, z: 4, core: 2. Of those that a mesh axis runs over, the one named last changes fastest.
Arguments:
- surface_points: float32 [3, 16384], P(None, ('vol', 'surf')), may hold values from -3 to 11
- surface_shift: float32 [3, 16384], P(None, ('vol', 'surf')), may hold values from -1.25 to 1.25
- facet_nodes: int32 [64, 3, 512], P(('vol', 'surf')), may hold values from 0 to 255, as said below
- volume_points: float32 [3, 65536], P(None, 'vol'), may hold values from -5 to 13
- near_wall: int32 [65536], P('vol'), may hold values from 0 to 1
- candidates: int32 [512, 16], P('vol'), may hold values from -1 to 63, as said below
Outputs:
- displacement: float32 [3, 65536], P(None, ('vol', 'surf'))
- wall_distance: float32 [65536], P(('vol', 'surf'))
The draws below stay inside these ranges and needn't reach their ends.
Inputs may be any that keep to these rules, and one draw needn't show every extreme that they name: Corner k of facet f of leaf l is surface node l * 256 + facet_nodes[l, k, f]; the three corners of a facet are distinct nodes of that leaf. `candidates`: in each row the real leaf ids come first, are distinct, and -1 fills the rest; every row holds at least one real id.
All inputs are finite; a program needn't handle non-finite values.
Results may differ from the reference program's by a relative error of at most 0.0003.
Values sent between devices are 32-bit elements; how exact they have to be, the bound alone decides.
No kernel may reach another device: no remote copies, remote signals or barrier semaphores. Data moves between devices by JAX's collectives and lax.ppermute only.
A program may use at most 64 MiB of HBM per device.

```python
import math
import jax
import jax.numpy as jnp
import numpy as np
from jax import lax

LEAF = 256
FL = 512
VB = 128
CAND = 16
LEAF_DEV = 2
V_DEV = 8192
LEAVES = 64
VNODES = 65536
VBLOCKS = 512


spacing = 0.1


def leaf_slots(key):
    perm_key = jax.random.fold_in(key, 101)
    leaf_keys = jax.random.split(perm_key, LEAVES)
    return jax.vmap(lambda leaf_key: jax.random.permutation(leaf_key, LEAF))(leaf_keys)


def grid_triangles():
    grid_side = math.isqrt(LEAF)
    columns = []
    for row_pos in range(grid_side - 1):
        for col_pos in range(grid_side - 1):
            corner_one = row_pos * grid_side + col_pos
            corner_two = corner_one + grid_side
            corner_three = corner_two + 1
            corner_four = corner_one + 1
            columns.append([corner_one, corner_two, corner_three])
            columns.append([corner_one, corner_three, corner_four])
    return np.array(columns, dtype=np.int32).T


def draw_facet_nodes(key, part):
    slot_of = leaf_slots(key)
    triangles = jnp.asarray(grid_triangles())
    tri_count = triangles.shape[1]
    padding = jax.random.randint(jax.random.fold_in(key, 202), (LEAVES, FL - tri_count), 0, tri_count)
    grid_ids = jnp.concatenate([jnp.broadcast_to(triangles[None], (LEAVES, 3, tri_count)), jnp.transpose(triangles[:, padding], (1, 0, 2))], axis=2)
    slot_table = jnp.broadcast_to(slot_of[:, None, :], (LEAVES, 3, LEAF))
    return jnp.take_along_axis(slot_table, grid_ids, axis=2).astype(jnp.int32)


def leaf_frames(key):
    geo_key = jax.random.fold_in(key, 303)
    key_root, key_frame, key_jitter = jax.random.split(geo_key, 3)
    root = jax.random.uniform(key_root, (LEAVES, 3), jnp.float32, 0.0, 8.0)
    raw_frame = jax.random.normal(key_frame, (LEAVES, 2, 3), jnp.float32)
    tangent_one = raw_frame[:, 0] / jnp.sqrt(jnp.sum(raw_frame[:, 0] ** 2, axis=1, keepdims=True))
    second_raw = raw_frame[:, 1] - jnp.sum(raw_frame[:, 1] * tangent_one, axis=1, keepdims=True) * tangent_one
    tangent_two = second_raw / jnp.sqrt(jnp.sum(second_raw ** 2, axis=1, keepdims=True))
    normal = jnp.cross(tangent_one, tangent_two)
    return (root, tangent_one, tangent_two, normal, key_jitter)


def candidate_table(key):
    cand_key = jax.random.fold_in(key, 606)
    key_count, key_start, key_coin, key_noise, key_anchor = jax.random.split(cand_key, 5)
    real_count = jax.random.randint(key_count, (VBLOCKS,), 1, CAND + 1)
    popular_start = jax.random.randint(key_start, (), 0, LEAVES)
    leaf_ids = jnp.arange(LEAVES, dtype=jnp.int32)
    in_window = (leaf_ids - popular_start) % LEAVES < 2 * LEAF_DEV
    popular_coin = jax.random.randint(key_coin, (VBLOCKS, LEAVES), 0, 10) < 5
    noise_draw = jax.random.randint(key_noise, (VBLOCKS, LEAVES), 0, 262144)
    boost_add = jnp.where(in_window[None, :] & popular_coin, 262144, 0)
    scores = (noise_draw + boost_add) * LEAVES + leaf_ids[None, :]
    top_values, top_ids = lax.top_k(scores, CAND)
    slot_ids = jnp.arange(CAND)[None, :]
    cand_table = jnp.where(slot_ids < real_count[:, None], top_ids, -1).astype(jnp.int32)
    anchor_slot = jax.random.randint(key_anchor, (VBLOCKS,), 0, 1048576) % real_count
    anchor_leaf = jnp.take_along_axis(top_ids, anchor_slot[:, None], axis=1)[:, 0].astype(jnp.int32)
    return (cand_table, anchor_leaf)


def draw_surface_points(key, part):
    slot_of = leaf_slots(key)
    root, tangent_one, tangent_two, normal, key_jitter = leaf_frames(key)
    grid_side = math.isqrt(LEAF)
    node_ids = jnp.arange(LEAF)
    along_one = (node_ids // grid_side).astype(jnp.float32) * spacing
    along_two = (node_ids % grid_side).astype(jnp.float32) * spacing
    jitter = jax.random.uniform(key_jitter, (LEAVES, LEAF, 3), jnp.float32, -0.05 * spacing, 0.05 * spacing)
    grid_pos = root[:, None, :] + along_one[None, :, None] * tangent_one[:, None, :] + along_two[None, :, None] * tangent_two[:, None, :] + jitter
    inverse = jnp.argsort(slot_of, axis=1)
    slot_pos = jnp.take_along_axis(grid_pos, jnp.broadcast_to(inverse[:, :, None], (LEAVES, LEAF, 3)), axis=1)
    return jnp.transpose(slot_pos.reshape(LEAVES * LEAF, 3)).astype(jnp.float32)


def draw_surface_shift(key, part):
    slot_of = leaf_slots(key)
    shift_key = jax.random.fold_in(key, 404)
    key_move, key_jitter, key_bend = jax.random.split(shift_key, 3)
    leaf_move = jnp.clip(0.4 * jax.random.normal(key_move, (LEAVES, 3), jnp.float32), -0.7, 0.7)
    bend = jax.random.uniform(key_bend, (LEAVES, 2, 3), jnp.float32, -1.0, 1.0)
    grid_side = math.isqrt(LEAF)
    node_ids = jnp.arange(LEAF)
    frac_one = (node_ids // grid_side).astype(jnp.float32) / (grid_side - 1) - 0.5
    frac_two = (node_ids % grid_side).astype(jnp.float32) / (grid_side - 1) - 0.5
    linear = 0.3 * (frac_one[None, :, None] * bend[:, 0][:, None, :] + frac_two[None, :, None] * bend[:, 1][:, None, :])
    rough = jax.random.uniform(key_jitter, (LEAVES, LEAF, 3), jnp.float32, -0.1, 0.1)
    grid_move = leaf_move[:, None, :] + linear + rough
    inverse = jnp.argsort(slot_of, axis=1)
    slot_move = jnp.take_along_axis(grid_move, jnp.broadcast_to(inverse[:, :, None], (LEAVES, LEAF, 3)), axis=1)
    return jnp.transpose(slot_move.reshape(LEAVES * LEAF, 3)).astype(jnp.float32)


def draw_volume_points(key, part):
    root, tangent_one, tangent_two, normal, key_jitter = leaf_frames(key)
    cand_table, anchor_leaf = candidate_table(key)
    place_key = jax.random.fold_in(key, 707)
    key_one, key_two, key_three = jax.random.split(place_key, 3)
    extent = (math.isqrt(LEAF) - 1) * spacing
    along_one = jax.random.uniform(key_one, (VBLOCKS, VB, 1), jnp.float32, 0.0, extent)
    along_two = jax.random.uniform(key_two, (VBLOCKS, VB, 1), jnp.float32, 0.0, extent)
    height = jax.random.uniform(key_three, (VBLOCKS, VB, 1), jnp.float32, 0.05, 4.0)
    anchor_base = root[anchor_leaf][:, None, :]
    node_pos = anchor_base + along_one * tangent_one[anchor_leaf][:, None, :] + along_two * tangent_two[anchor_leaf][:, None, :] + height * normal[anchor_leaf][:, None, :]
    return jnp.transpose(node_pos.reshape(VNODES, 3)).astype(jnp.float32)


def draw_near_wall(key, part):
    flag_key = jax.random.fold_in(key, 505)
    key_level, key_block, key_node = jax.random.split(flag_key, 3)
    vol_count = VNODES // V_DEV
    blocks_dev = V_DEV // VB
    near_level = jax.random.randint(key_level, (vol_count,), 2, 7)
    block_draw = jax.random.randint(key_block, (VBLOCKS,), 0, 20)
    block_ids = jnp.arange(VBLOCKS)
    owner_dev = block_ids // blocks_dev
    first_half = block_ids % blocks_dev < blocks_dev // 2
    threshold = jnp.where(first_half, 3 * near_level[owner_dev], near_level[owner_dev])
    block_near = block_draw < threshold
    node_pick = jax.random.randint(key_node, (VNODES,), 0, 4) < 3
    return (jnp.repeat(block_near, VB) & node_pick).astype(jnp.int32)


def draw_candidates(key, part):
    cand_table, anchor_leaf = candidate_table(key)
    return cand_table


def setup_inputs(seed: int = 0) -> dict:
    streams_of = jax.random.split(jax.random.key(seed), 7)
    surface_points = draw_surface_points(jax.random.fold_in(streams_of[6], 71), 0)
    surface_shift = draw_surface_shift(jax.random.fold_in(streams_of[6], 71), 0)
    facet_nodes = draw_facet_nodes(jax.random.fold_in(streams_of[6], 71), 0)
    volume_points = draw_volume_points(jax.random.fold_in(streams_of[6], 71), 0)
    near_wall = draw_near_wall(jax.random.fold_in(streams_of[6], 71), 0)
    candidates = draw_candidates(jax.random.fold_in(streams_of[6], 71), 0)
    return dict(surface_points=surface_points, surface_shift=surface_shift, facet_nodes=facet_nodes, volume_points=volume_points, near_wall=near_wall, candidates=candidates)


smoothing = 0.01
big_value = 1e+30

def minus3(first_vec, second_vec):
    return [first_vec[0] - second_vec[0], first_vec[1] - second_vec[1], first_vec[2] - second_vec[2]]

def dot3(first_vec, second_vec):
    return first_vec[0] * second_vec[0] + first_vec[1] * second_vec[1] + first_vec[2] * second_vec[2]

def cross3(first_vec, second_vec):
    return [first_vec[1] * second_vec[2] - first_vec[2] * second_vec[1], first_vec[2] * second_vec[0] - first_vec[0] * second_vec[2], first_vec[0] * second_vec[1] - first_vec[1] * second_vec[0]]

def segment_squares(offset_vec, edge_vec, inverse_length):
    fraction = jnp.clip(dot3(offset_vec, edge_vec) * inverse_length, 0.0, 1.0)
    remain = [offset_vec[0] - fraction * edge_vec[0], offset_vec[1] - fraction * edge_vec[1], offset_vec[2] - fraction * edge_vec[2]]
    return dot3(remain, remain)

def facet_squares(points, corners):
    probe_point = [points[..., 0, :, None], points[..., 1, :, None], points[..., 2, :, None]]
    vert_a = [corners[..., 0, None, :], corners[..., 1, None, :], corners[..., 2, None, :]]
    vert_b = [corners[..., 3, None, :], corners[..., 4, None, :], corners[..., 5, None, :]]
    vert_c = [corners[..., 6, None, :], corners[..., 7, None, :], corners[..., 8, None, :]]
    edge_ab = minus3(vert_b, vert_a)
    edge_bc = minus3(vert_c, vert_b)
    edge_ca = minus3(vert_a, vert_c)
    normal = cross3(edge_ab, minus3(vert_c, vert_a))
    inverse_normal = 1.0 / dot3(normal, normal)
    side_ab = cross3(normal, edge_ab)
    side_bc = cross3(normal, edge_bc)
    side_ca = cross3(normal, edge_ca)
    from_a = minus3(probe_point, vert_a)
    from_b = minus3(probe_point, vert_b)
    from_c = minus3(probe_point, vert_c)
    inside = (dot3(from_a, side_ab) >= 0.0) & (dot3(from_b, side_bc) >= 0.0) & (dot3(from_c, side_ca) >= 0.0)
    height = dot3(from_a, normal)
    plane_sq = height * height * inverse_normal
    edge_sq = jnp.minimum(segment_squares(from_a, edge_ab, 1.0 / dot3(edge_ab, edge_ab)), segment_squares(from_b, edge_bc, 1.0 / dot3(edge_bc, edge_bc)))
    edge_sq = jnp.minimum(edge_sq, segment_squares(from_c, edge_ca, 1.0 / dot3(edge_ca, edge_ca)))
    return jnp.where(inside, plane_sq, edge_sq)

def inverse_square(points, others):
    distance_sq = (others[..., 0, :, None] - points[..., 0, None, :]) ** 2
    distance_sq = distance_sq + (others[..., 1, :, None] - points[..., 1, None, :]) ** 2
    distance_sq = distance_sq + (others[..., 2, :, None] - points[..., 2, None, :]) ** 2
    inverse = 1.0 / (distance_sq + smoothing)
    return inverse * inverse

def weigh_sums(weight, shift):
    return jnp.stack([lax.optimization_barrier(jnp.sum(weight * shift[..., 0, :, None], axis=-2)), lax.optimization_barrier(jnp.sum(weight * shift[..., 1, :, None], axis=-2)), lax.optimization_barrier(jnp.sum(weight * shift[..., 2, :, None], axis=-2)), lax.optimization_barrier(jnp.sum(weight, axis=-2))], axis=-2)

def corner_table(moved_nodes, facet_nodes):
    leaves = facet_nodes.shape[0]
    per_leaf = jnp.moveaxis(moved_nodes.reshape(3, leaves, -1), 1, 0)
    pieces = []
    for corner in range(3):
        gather_index = jnp.broadcast_to(facet_nodes[:, corner:corner + 1, :], (leaves, 3, facet_nodes.shape[2]))
        pieces.append(jnp.take_along_axis(per_leaf, gather_index, axis=2))
    return jnp.concatenate(pieces, axis=1)

def reference(surface_points, surface_shift, facet_nodes, volume_points, near_wall, candidates):
    leaves = facet_nodes.shape[0]
    leaf_len = surface_points.shape[1] // leaves
    total_vol = volume_points.shape[1]
    block_len = total_vol // candidates.shape[0]
    leaf_points = jnp.moveaxis(surface_points.reshape(3, leaves, leaf_len), 1, 0)
    leaf_shift = jnp.moveaxis(surface_shift.reshape(3, leaves, leaf_len), 1, 0)
    centers = jnp.transpose(lax.optimization_barrier(jnp.mean(leaf_points, axis=2)))
    center_shift = jnp.transpose(lax.optimization_barrier(jnp.mean(leaf_shift, axis=2)))
    leaf_ids = jnp.arange(leaves, dtype=jnp.int32)
    block_points = jnp.moveaxis(volume_points.reshape(3, -1, block_len), 1, 0)

    def weigh(packed):
        points_here, cands_here = packed
        safe_rows = jnp.maximum(cands_here, 0).astype(jnp.int32)
        near_weight = inverse_square(points_here[None], leaf_points[safe_rows])
        near_terms = weigh_sums(near_weight, leaf_shift[safe_rows])
        near_part = lax.optimization_barrier(jnp.sum(jnp.where((cands_here >= 0)[:, None, None], near_terms, 0.0), axis=0))
        listed = jnp.any(cands_here[:, None] == leaf_ids[None, :], axis=0)
        far_weight = inverse_square(points_here, centers) * leaf_len
        far_weight = jnp.where(listed[:, None], 0.0, far_weight)
        far_part = weigh_sums(far_weight, center_shift)
        return near_part + far_part
    weighted = lax.map(weigh, (block_points, candidates))
    weighted = jnp.moveaxis(weighted, 0, 1).reshape(4, total_vol)
    displacement = weighted[:3] / weighted[3:4]
    moved_volume = volume_points + displacement
    moved_surface = surface_points + surface_shift
    leaf_table = corner_table(moved_surface, facet_nodes)
    moved_blocks = jnp.moveaxis(moved_volume.reshape(3, -1, block_len), 1, 0)
    flag_blocks = near_wall.reshape(-1, block_len)

    def one_block(packed):
        points_here, flags_here, cands_here = packed

        def compute(unused_arg):
            corners = leaf_table[jnp.maximum(cands_here, 0)]
            squared = facet_squares(points_here[None], corners)
            squared = jnp.where(cands_here[:, None, None] >= 0, squared, big_value)
            return lax.optimization_barrier(jnp.min(squared, axis=(0, 2)))

        def skipped(unused_arg):
            return jnp.full((block_len,), big_value, jnp.float32)
        return lax.cond(jnp.max(flags_here) > 0, compute, skipped, 0)
    nearest = lax.map(one_block, (moved_blocks, flag_blocks, candidates)).reshape(-1)
    wall_distance = jnp.where(near_wall == 1, jnp.sqrt(nearest), 0.0)
    return (displacement, wall_distance)
```

```python
import functools

import jax
import jax.numpy as jnp
from jax import lax
from jax.experimental import pallas as pl
from jax.experimental.pallas import tpu as pltpu
from jax.sharding import PartitionSpec as P

smoothing = 0.01
big_value = 1e30
LANES = 128
COEFS = 24


def prep_kernel(points_ref, shift_ref, facets_ref, out_ref):
    leaf_dev, corners, facet_len = facets_ref.shape
    leaf_len = points_ref.shape[1] // leaf_dev
    halves, chunks = leaf_len // LANES, facet_len // LANES
    tail = jnp.where(lax.broadcasted_iota(jnp.int32, (2, LANES), 0) == 0, 1.0, 0.0)
    for leaf in range(leaf_dev):
        for half in range(halves):
            row = (leaf * halves + half) * 8
            lanes = pl.ds((leaf * halves + half) * LANES, LANES)
            out_ref[0, row : row + 3, :] = points_ref[:, lanes]
            out_ref[0, row + 3 : row + 6, :] = shift_ref[:, lanes]
            out_ref[0, row + 6 : row + 8, :] = tail
    base = leaf_dev * halves * 8
    for leaf in range(leaf_dev):
        for chunk in range(chunks):
            ids = facets_ref[leaf, :, chunk * LANES : (chunk + 1) * LANES].astype(jnp.float32)
            for corner in range(corners):
                row = base + (corner * leaf_dev + leaf) * chunks + chunk
                out_ref[0, row : row + 1, :] = ids[corner : corner + 1, :]


def split3(value):
    first = value.astype(jnp.bfloat16)
    rest = value - first.astype(jnp.float32)
    second = rest.astype(jnp.bfloat16)
    third = (rest - second.astype(jnp.float32)).astype(jnp.bfloat16)
    return first, second, third


def near_kernel(
    leaf_dev, halves, meta_ref, rank_ref, low_ref, high_ref, volume_ref, disp_ref, moved_ref,
    nodes, sums_table, moments, spread,
):
    half_dev = low_ref.shape[0]
    leaves = nodes.shape[0]
    blocks = disp_ref.shape[1] // LANES
    leaf_len = halves * LANES
    lane_ids = lax.broadcasted_iota(jnp.int32, (8, LANES), 1)
    groups = moments.shape[1] // LANES
    moments[...] = jnp.zeros_like(moments)

    def load_device(dev, src_ref, offset):
        for leaf in range(leaf_dev):
            place = (dev + offset) * leaf_dev + leaf
            tiles = []
            for half in range(halves):
                row = (leaf * halves + half) * 8
                tile = src_ref[dev, row : row + 8, :]
                nodes[place, half] = tile
                tiles.append(tile)
            whole = jnp.concatenate(tiles, axis=1)
            parts = split3(whole)
            sums_table[place] = jnp.concatenate(
                [part.astype(jnp.float32) for part in parts], axis=0
            ).astype(jnp.bfloat16)
            total = functools.reduce(lambda a, b: a + b, tiles)
            total = jnp.sum(total, axis=1, keepdims=True)
            group = place // LANES
            lanes = pl.ds(pl.multiple_of(group * LANES, LANES), LANES)
            moments[:, lanes] = jnp.where(
                lane_ids == place - group * LANES, total, moments[:, lanes]
            )

    def load_low(dev, carry):
        load_device(dev, low_ref, 0)
        return carry

    def load_high(dev, carry):
        load_device(dev, high_ref, half_dev)
        return carry

    lax.fori_loop(0, half_dev, load_low, 0)
    lax.fori_loop(0, half_dev, load_high, 0)

    def weigh(x_row, y_row, z_row, sums, acc, mask):
        tiles_high, tiles_low = [], []
        width = x_row.shape[1] // LANES
        for tile in range(width):
            lanes = slice(tile * LANES, (tile + 1) * LANES)
            dx = x_row[:, lanes] - spread[0]
            dy = y_row[:, lanes] - spread[1]
            dz = z_row[:, lanes] - spread[2]
            inverse = 1.0 / (dx * dx + dy * dy + dz * dz + smoothing)
            weight = inverse * inverse
            if mask is not None:
                weight = weight * mask[:, lanes]
            high = weight.astype(jnp.bfloat16)
            low = (weight - high.astype(jnp.float32)).astype(jnp.bfloat16)
            tiles_high.append(high)
            tiles_low.append(low)
        dims = (((1,), (1,)), ((), ()))
        high = jnp.concatenate(tiles_high, axis=1)
        low = jnp.concatenate(tiles_low, axis=1)
        acc = acc + lax.dot_general(high, sums, dims, preferred_element_type=jnp.float32)
        return acc + lax.dot_general(low, sums, dims, preferred_element_type=jnp.float32)

    def one_block(block, carry):
        start = pl.multiple_of((rank_ref[0] * blocks + block) * LANES, LANES)
        here = volume_ref[:, pl.ds(start, LANES)]
        columns = jnp.transpose(
            jnp.concatenate([here, jnp.zeros((5, LANES), jnp.float32)], axis=0)
        )
        for axis in range(3):
            spread[axis] = jnp.broadcast_to(columns[:, axis : axis + 1], (LANES, LANES))
        count = meta_ref[block, 0]

        def far_group(group, acc):
            lanes = pl.ds(pl.multiple_of(group * LANES, LANES), LANES)
            place = lane_ids[:1] + group * LANES
            mask = jnp.where(place < leaves, 1.0, 0.0)

            def drop(slot, mask):
                return jnp.where(place == meta_ref[block, 2 + slot], 0.0, mask)

            mask = lax.fori_loop(0, count, drop, mask)
            tile = moments[:, lanes]
            center = tile * (1.0 / leaf_len)
            sums = jnp.concatenate(
                [part.astype(jnp.float32) for part in split3(tile)], axis=0
            ).astype(jnp.bfloat16)
            return weigh(center[0:1], center[1:2], center[2:3], sums, acc, mask)

        acc = jnp.zeros((LANES, COEFS), jnp.float32)
        acc = lax.fori_loop(0, groups, far_group, acc)

        def near_leaf(slot, acc):
            place = meta_ref[block, 2 + slot]
            rows = [
                jnp.concatenate([nodes[place, half, axis : axis + 1, :] for half in range(halves)], axis=1)
                for axis in range(3)
            ]
            return weigh(*rows, sums_table[place], acc, None)

        acc = lax.fori_loop(0, count, near_leaf, acc)
        sums = jnp.transpose(acc)
        sums = sums[0:8] + sums[8:16] + sums[16:24]
        moved_by = sums[3:6] / sums[6:7]
        lanes = pl.ds(pl.multiple_of(block * LANES, LANES), LANES)
        disp_ref[:, lanes] = moved_by
        moved_ref[:, lanes] = here + moved_by
        return carry

    lax.fori_loop(0, blocks, one_block, 0)


def cross(a, b):
    return (a[1] * b[2] - a[2] * b[1], a[2] * b[0] - a[0] * b[2], a[0] * b[1] - a[1] * b[0])


def dot(a, b):
    return a[0] * b[0] + a[1] * b[1] + a[2] * b[2]


def wall_kernel(
    leaf_dev, halves, chunks, meta_ref, rank_ref, low_ref, high_ref, moved_ref, flags_ref, wall_ref,
    coefs, sphere_tiles, spheres, spread, nearest, active, active_scalars, work, sem,
):
    half_dev = low_ref.shape[0]
    rows = leaf_dev * chunks
    blocks = wall_ref.shape[0]
    columns_len = spheres.shape[1]
    groups = columns_len // LANES
    base = leaf_dev * halves * 8
    lane_ids = lax.broadcasted_iota(jnp.int32, (rows, LANES), 1)
    row_ids = lax.broadcasted_iota(jnp.int32, (rows, LANES), 0)
    per_group = LANES // rows
    sphere_tiles[...] = jnp.zeros_like(sphere_tiles)

    def load_device(dev, src_ref, offset):
        place = dev + offset
        moved = []
        for axis in range(3):
            parts = []
            for half in range(halves):
                pieces = []
                for leaf in range(leaf_dev):
                    row = (leaf * halves + half) * 8
                    line = src_ref[dev, row + axis : row + axis + 1, :]
                    line = line + src_ref[dev, row + 3 + axis : row + 4 + axis, :]
                    pieces.append(jnp.broadcast_to(line, (chunks, LANES)))
                parts.append(jnp.concatenate(pieces, axis=0))
            moved.append(parts)
        corners = []
        for corner in range(3):
            ids = src_ref[dev, base + corner * rows : base + (corner + 1) * rows, :].astype(jnp.int32)
            lane = ids & (LANES - 1)
            vertex = []
            for axis in range(3):
                value = jnp.take_along_axis(moved[axis][0], lane, axis=1)
                for half in range(1, halves):
                    other = jnp.take_along_axis(moved[axis][half], lane, axis=1)
                    value = jnp.where(ids >= half * LANES, other, value)
                vertex.append(value)
            corners.append(vertex)
        a, b, c = corners
        ab = [b[k] - a[k] for k in range(3)]
        ac = [c[k] - a[k] for k in range(3)]
        length = jnp.sqrt(dot(ab, ab))
        scale = 1.0 / length
        along = [v * scale for v in ab]
        normal = cross(ab, ac)
        scale = 1.0 / jnp.sqrt(dot(normal, normal))
        normal = [v * scale for v in normal]
        across = cross(normal, along)
        cx, cy = dot(ac, along), dot(ac, across)
        bx = cx - length
        length_b = jnp.sqrt(bx * bx + cy * cy)
        scale = 1.0 / length_b
        bdx, bdy = bx * scale, cy * scale
        length_c = jnp.sqrt(cx * cx + cy * cy)
        scale = 1.0 / length_c
        cdx, cdy = cx * scale, cy * scale
        values = a + along + list(across) + list(normal)
        values += [
            0.5 * length, bdx, bdy, -length * bdx - 0.5 * length_b, length * bdy, 0.5 * length_b,
            cdx, cdy, 0.5 * length_c,
        ]
        for index, value in enumerate(values):
            coefs[place, index] = value
        low = [jnp.min(jnp.minimum(jnp.minimum(a[k], b[k]), c[k]), axis=1, keepdims=True) for k in range(3)]
        high = [jnp.max(jnp.maximum(jnp.maximum(a[k], b[k]), c[k]), axis=1, keepdims=True) for k in range(3)]
        center = [0.5 * (low[k] + high[k]) for k in range(3)]
        squares = []
        for vertex in corners:
            diff = [vertex[k] - center[k] for k in range(3)]
            squares.append(dot(diff, diff))
        far = jnp.max(jnp.maximum(jnp.maximum(squares[0], squares[1]), squares[2]), axis=1, keepdims=True)
        close = jnp.min(jnp.minimum(jnp.minimum(squares[0], squares[1]), squares[2]), axis=1, keepdims=True)
        group = place // per_group
        here = lane_ids - row_ids == (place - group * per_group) * rows
        for index, value in enumerate(center + [jnp.sqrt(far), jnp.sqrt(close)]):
            sphere_tiles[group, index] = jnp.where(here, value, sphere_tiles[group, index])

    def load_low(dev, carry):
        load_device(dev, low_ref, 0)
        return carry

    def load_high(dev, carry):
        load_device(dev, high_ref, half_dev)
        return carry

    lax.fori_loop(0, half_dev, load_low, 0)
    lax.fori_loop(0, half_dev, load_high, 0)
    for group in range(groups):
        for index in range(5):
            spheres[index : index + 1, group * LANES : (group + 1) * LANES] = jnp.sum(
                sphere_tiles[group, index], axis=0, keepdims=True
            )

    def columns_of(block):
        start = pl.multiple_of(block * LANES, LANES)
        here = moved_ref[:, pl.ds(start, LANES)]
        flags = flags_ref[pl.ds(rank_ref[0] * blocks + block, 1), :].astype(jnp.float32)
        return jnp.transpose(
            jnp.concatenate([here, flags, jnp.zeros((4, LANES), jnp.float32)], axis=0)
        )

    lane_row = lax.broadcasted_iota(jnp.int32, (1, LANES), 1)

    def find_active(block, carry):
        count = meta_ref[block, 0]

        @pl.when(meta_ref[block, 1] > 0)
        def _():
            columns = columns_of(block)
            px, py, pz, flag = (columns[:, k : k + 1] for k in range(4))

            def distances(group):
                lanes = pl.ds(pl.multiple_of(group * LANES, LANES), LANES)
                tile = spheres[:, lanes]
                dx, dy, dz = tile[0:1] - px, tile[1:2] - py, tile[2:3] - pz
                place = (lane_row + group * LANES) // chunks

                def mark(slot, listed):
                    return jnp.where(place == meta_ref[block, 2 + slot], 1.0, listed)

                listed = lax.fori_loop(0, count, mark, jnp.zeros((1, LANES), jnp.float32))
                return jnp.sqrt(dx * dx + dy * dy + dz * dz), tile, listed, lanes

            def upper(group, best):
                distance, tile, listed, lanes = distances(group)
                bound = jnp.where(listed > 0.0, distance + tile[4:5], big_value)
                return jnp.minimum(best, bound)

            best = lax.fori_loop(0, groups, upper, jnp.full((LANES, LANES), big_value, jnp.float32))
            best = jnp.min(best, axis=1, keepdims=True)
            limit = jnp.where(flag > 0.0, best * 1.0001 + 1e-4, -big_value)

            def lower(group, carry):
                distance, tile, listed, lanes = distances(group)
                keep = jnp.where(distance - tile[3:4] <= limit, 1.0, 0.0)
                keep = jnp.max(keep, axis=0, keepdims=True) * listed
                active[pl.ds(group * blocks + block, 1), :] = keep.astype(jnp.int32)
                return carry

            lax.fori_loop(0, groups, lower, 0)

        return carry

    lax.fori_loop(0, blocks, find_active, 0)
    copy = pltpu.make_async_copy(active, active_scalars, sem)
    copy.start()
    copy.wait()

    def one_block(block, carry):
        count = meta_ref[block, 0]
        wall_ref[pl.ds(block, 1), :] = jnp.zeros((1, LANES), jnp.float32)

        @pl.when(meta_ref[block, 1] > 0)
        def _():
            columns = columns_of(block)
            for axis in range(3):
                spread[axis] = jnp.broadcast_to(columns[:, axis : axis + 1], (LANES, LANES))
            nearest[...] = jnp.full((LANES, LANES), big_value, jnp.float32)

            def list_leaf(slot, found):
                first = meta_ref[block, 2 + slot] * chunks
                row, lane = first // LANES * blocks + block, first % LANES
                for chunk in range(chunks):
                    work[found] = first + chunk
                    found = found + active_scalars[row, lane + chunk]
                return found

            found = lax.fori_loop(0, count, list_leaf, 0)

            def one_item(item, carry):
                column = work[item]
                dev = column // rows
                row = column - dev * rows
                value = [
                    jnp.broadcast_to(coefs[dev, k, pl.ds(row, 1), :], (8, LANES)) for k in range(21)
                ]
                ax, ay, az, ex, ey, ez, mx, my, mz, nx, ny, nz = value[:12]
                half_a, bdx, bdy, b_shift, b_side, half_b, cdx, cdy, half_c = value[12:]
                for step in range(LANES // 8):
                    part = slice(step * 8, step * 8 + 8)
                    qx, qy, qz = spread[0, part] - ax, spread[1, part] - ay, spread[2, part] - az
                    u = qx * ex + qy * ey + qz * ez
                    w = qx * mx + qy * my + qz * mz
                    h = qx * nx + qy * ny + qz * nz
                    side_b = w * bdx - u * bdy + b_side
                    side_c = u * cdy - w * cdx
                    over_a = jnp.maximum(jnp.abs(u - half_a) - half_a, 0.0)
                    over_b = jnp.maximum(jnp.abs(u * bdx + w * bdy + b_shift) - half_b, 0.0)
                    over_c = jnp.maximum(jnp.abs(u * cdx + w * cdy - half_c) - half_c, 0.0)
                    edge = jnp.minimum(w * w + over_a * over_a, side_b * side_b + over_b * over_b)
                    edge = jnp.minimum(edge, side_c * side_c + over_c * over_c)
                    inside = jnp.minimum(jnp.minimum(w, side_b), side_c) >= 0.0
                    square = jnp.where(inside, 0.0, edge) + h * h
                    nearest[part] = jnp.minimum(nearest[part], square)
                return carry

            lax.fori_loop(0, found, one_item, 0)
            square = jnp.min(jnp.transpose(nearest[...]), axis=0, keepdims=True)
            flags = flags_ref[pl.ds(rank_ref[0] * blocks + block, 1), :]
            wall_ref[pl.ds(block, 1), :] = jnp.where(flags == 1, jnp.sqrt(square), 0.0)

        return carry

    lax.fori_loop(0, blocks, one_block, 0)


def gather_order(vol_count, surf_count):
    steps = []
    bit = surf_count // 2
    while bit >= 1:
        steps.append(("surf", bit))
        bit //= 2
    bit = vol_count // 2
    while bit >= 1:
        steps.append(("vol", bit))
        bit //= 2
    return steps


def body(surface_points, surface_shift, facet_nodes, volume_points, near_wall, candidates):
    surf_count, vol_count = lax.axis_size("surf"), lax.axis_size("vol")
    sizes = {"surf": surf_count, "vol": vol_count}
    ranks = {"surf": lax.axis_index("surf"), "vol": lax.axis_index("vol")}
    leaf_dev, _, facet_len = facet_nodes.shape
    leaf_len = surface_points.shape[1] // leaf_dev
    halves, chunks = leaf_len // LANES, facet_len // LANES
    devices = surf_count * vol_count
    leaves = devices * leaf_dev
    slots = candidates.shape[1]
    blocks = candidates.shape[0] // surf_count
    share_len = volume_points.shape[1] // surf_count
    rows = leaf_dev * chunks
    payload_rows = leaf_dev * halves * 8 + 3 * rows
    vmem = pl.BlockSpec(memory_space=pltpu.VMEM)
    smem = pl.BlockSpec(memory_space=pltpu.SMEM)
    params = pltpu.CompilerParams(vmem_limit_bytes=60 * 1024 * 1024)

    held = pl.pallas_call(
        prep_kernel,
        out_shape=jax.ShapeDtypeStruct((1, payload_rows, LANES), jnp.float32),
        in_specs=[vmem] * 3,
        out_specs=vmem,
    )(surface_points, surface_shift, facet_nodes)
    steps = gather_order(vol_count, surf_count)
    for index, (axis, bit) in enumerate(steps):
        pairs = [(source, source ^ bit) for source in range(sizes[axis])]
        arrived = lax.ppermute(held, axis, pairs)
        if index < len(steps) - 1:
            held = jnp.concatenate([held, arrived], axis=0)

    own = lax.dynamic_slice_in_dim(candidates, ranks["surf"] * blocks, blocks, 0)
    owner = jnp.maximum(own, 0) // leaf_dev
    apart = {"surf": (owner % surf_count) ^ ranks["surf"], "vol": (owner // surf_count) ^ ranks["vol"]}
    place = jnp.zeros_like(own)
    for index, (axis, bit) in enumerate(steps):
        place = place + jnp.where((apart[axis] & bit) != 0, 1 << index, 0)
    place = place * leaf_dev + jnp.maximum(own, 0) % leaf_dev
    count = jnp.sum((own >= 0).astype(jnp.int32), axis=1, keepdims=True)
    flag_rows = near_wall.reshape(-1, LANES)
    own_flags = lax.dynamic_slice_in_dim(flag_rows, ranks["surf"] * blocks, blocks, 0)
    near = jnp.max(own_flags, axis=1, keepdims=True)
    meta = jnp.concatenate([count, near, place], axis=1)
    rank = ranks["surf"].reshape(1).astype(jnp.int32)

    groups = -(-leaves // LANES)
    disp, moved = pl.pallas_call(
        functools.partial(near_kernel, leaf_dev, halves),
        out_shape=[jax.ShapeDtypeStruct((3, share_len), jnp.float32)] * 2,
        in_specs=[smem, smem, vmem, vmem, vmem],
        out_specs=[vmem, vmem],
        scratch_shapes=[
            pltpu.VMEM((leaves, halves, 8, LANES), jnp.float32),
            pltpu.VMEM((leaves, COEFS, leaf_len), jnp.bfloat16),
            pltpu.VMEM((8, groups * LANES), jnp.float32),
            pltpu.VMEM((3, LANES, LANES), jnp.float32),
        ],
        compiler_params=params,
    )(meta, rank, held, arrived, volume_points)
    columns_len = devices * rows
    column_groups = columns_len // LANES
    wall = pl.pallas_call(
        functools.partial(wall_kernel, leaf_dev, halves, chunks),
        out_shape=jax.ShapeDtypeStruct((blocks, LANES), jnp.float32),
        in_specs=[smem, smem, vmem, vmem, vmem, vmem],
        out_specs=vmem,
        scratch_shapes=[
            pltpu.VMEM((devices, COEFS, rows, LANES), jnp.float32),
            pltpu.VMEM((column_groups, 5, rows, LANES), jnp.float32),
            pltpu.VMEM((8, columns_len), jnp.float32),
            pltpu.VMEM((3, LANES, LANES), jnp.float32),
            pltpu.VMEM((LANES, LANES), jnp.float32),
            pltpu.VMEM((column_groups * blocks, LANES), jnp.int32),
            pltpu.SMEM((column_groups * blocks, LANES), jnp.int32),
            pltpu.SMEM((slots * chunks + 1,), jnp.int32),
            pltpu.SemaphoreType.DMA,
        ],
        compiler_params=params,
    )(meta, rank, held, arrived, moved, flag_rows)
    return (disp, wall.reshape(-1))


def solution(mesh):
    placed = (
        P(None, ("vol", "surf")),
        P(None, ("vol", "surf")),
        P(("vol", "surf"), None, None),
        P(None, "vol"),
        P("vol"),
        P("vol", None),
    )
    return jax.shard_map(
        body,
        mesh=mesh,
        in_specs=placed,
        out_specs=(P(None, ("vol", "surf")), P(("vol", "surf"))),
        check_vma=False,
    )
```

```python
import functools

import jax
import jax.numpy as jnp
from jax import lax
from jax.experimental import pallas as pl
from jax.experimental.pallas import tpu as pltpu
from jax.sharding import PartitionSpec as P

smoothing = 0.01
big_value = 1e30
LANES = 128
COEFS = 24


def prep_kernel(points_ref, shift_ref, facets_ref, out_ref):
    leaf_dev, corners, facet_len = facets_ref.shape
    leaf_len = points_ref.shape[1] // leaf_dev
    halves, chunks = leaf_len // LANES, facet_len // LANES
    tail = jnp.where(lax.broadcasted_iota(jnp.int32, (2, LANES), 0) == 0, 1.0, 0.0)
    for leaf in range(leaf_dev):
        for half in range(halves):
            row = (leaf * halves + half) * 8
            lanes = pl.ds((leaf * halves + half) * LANES, LANES)
            out_ref[0, row : row + 3, :] = points_ref[:, lanes]
            out_ref[0, row + 3 : row + 6, :] = shift_ref[:, lanes]
            out_ref[0, row + 6 : row + 8, :] = tail
    base = leaf_dev * halves * 8
    for leaf in range(leaf_dev):
        for chunk in range(chunks):
            ids = facets_ref[leaf, :, chunk * LANES : (chunk + 1) * LANES].astype(jnp.float32)
            for corner in range(corners):
                row = base + (corner * leaf_dev + leaf) * chunks + chunk
                out_ref[0, row : row + 1, :] = ids[corner : corner + 1, :]


def split3(value):
    first = value.astype(jnp.bfloat16)
    rest = value - first.astype(jnp.float32)
    second = rest.astype(jnp.bfloat16)
    third = (rest - second.astype(jnp.float32)).astype(jnp.bfloat16)
    return first, second, third


def stack6(tiles, order):
    return jnp.concatenate([tiles[k] for k in order], axis=0)


def parts3(tile):
    return [part.astype(jnp.float32) for part in split3(tile)]


LEFT = (0, 0, 0, 1, 1, 2)
RIGHT = (0, 1, 2, 0, 1, 0)


def near_kernel(
    leaf_dev, halves, meta_ref, rank_ref, low_ref, high_ref, volume_ref, disp_ref, moved_ref,
    nodes, rights, middles, moments, acc, ready, lefts,
):
    half_dev = low_ref.shape[0]
    leaves = nodes.shape[0] - 1
    blocks = disp_ref.shape[1] // LANES
    leaf_len = halves * LANES
    slots = meta_ref.shape[1] - 2
    lane_ids = lax.broadcasted_iota(jnp.int32, (8, LANES), 1)
    row_ids = lax.broadcasted_iota(jnp.int32, (8, LANES), 0)
    groups = moments.shape[1] // LANES

    def right_side(tile, center):
        rows = lax.broadcasted_iota(jnp.int32, tile.shape, 0)
        apart = jnp.where(rows < 3, tile - center, 0.0)
        norm = jnp.sum(apart * apart, axis=0, keepdims=True) + smoothing
        right = jnp.where(rows == 3, 1.0, jnp.where(rows == 4, norm, -2.0 * apart))
        return stack6(parts3(right), RIGHT).astype(jnp.bfloat16)

    def left_side(tile, center):
        offset = jnp.where(row_ids < 3, tile - center, 0.0)
        norm = jnp.sum(offset * offset, axis=0, keepdims=True)
        left = jnp.where(row_ids == 3, norm, jnp.where(row_ids == 4, 1.0, offset))
        return jnp.transpose(stack6(parts3(left), LEFT)).astype(jnp.bfloat16)

    def squares(left, right):
        return jnp.dot(left, right, preferred_element_type=jnp.float32)

    def point_tile(block):
        start = pl.multiple_of((rank_ref[0] * blocks + block) * LANES, LANES)
        here = volume_ref[:, pl.ds(start, LANES)]
        return jnp.concatenate([here, jnp.zeros((5, LANES), jnp.float32)], axis=0)

    moments[...] = jnp.zeros_like(moments)
    nodes[leaves] = jnp.zeros_like(nodes[leaves])
    middles[leaves] = jnp.zeros_like(middles[leaves])
    away = lax.broadcasted_iota(jnp.int32, (48, leaf_len), 0) == 4
    rights[leaves] = jnp.where(away, 1e25, 0.0).astype(jnp.bfloat16)

    def load_device(dev, src_ref, offset):
        for leaf in range(leaf_dev):
            place = (dev + offset) * leaf_dev + leaf
            tiles = []
            for half in range(halves):
                row = (leaf * halves + half) * 8
                tiles.append(src_ref[dev, row : row + 8, :])
            whole = jnp.concatenate(tiles, axis=1)
            nodes[place] = whole
            total = functools.reduce(lambda a, b: a + b, tiles)
            total = jnp.sum(total, axis=1, keepdims=True)
            center = total * (1.0 / leaf_len)
            middles[place] = jnp.broadcast_to(center, (8, LANES))
            rights[place] = right_side(whole, center)
            group = place // LANES
            lanes = pl.ds(pl.multiple_of(group * LANES, LANES), LANES)
            moments[:, lanes] = jnp.where(
                lane_ids == place - group * LANES, total, moments[:, lanes]
            )

    def load_low(dev, carry):
        load_device(dev, low_ref, 0)
        return carry

    def load_high(dev, carry):
        load_device(dev, high_ref, half_dev)
        return carry

    lax.fori_loop(0, half_dev, load_low, 0, unroll=2)
    lax.fori_loop(0, half_dev, load_high, 0, unroll=2)

    def far_blocks(step, carry):
        here = [step * 2 + k for k in range(2)]
        centers, lefts = [], []
        for block in here:
            tile = point_tile(block)
            center = jnp.sum(tile, axis=1, keepdims=True) * (1.0 / LANES)
            centers.append(center)
            lefts.append(left_side(tile, center))
        for group in range(groups):
            tile = moments[:, group * LANES : (group + 1) * LANES]
            place = lane_ids[:1] + group * LANES
            found = [
                squares(lefts[k], right_side(tile * (1.0 / leaf_len), centers[k])) for k in range(2)
            ]
            for k in range(2):
                listed = place >= leaves
                for slot in range(slots):
                    listed = listed | (place == meta_ref[here[k], 2 + slot])
                mask = jnp.where(listed, 0.0, 1.0)
                inverse = 1.0 / found[k]
                weight = inverse * inverse * mask
                for index in range(4):
                    term = weight * tile[3 + index : 4 + index]
                    if group > 0:
                        term = term + acc[here[k], index]
                    acc[here[k], index] = term
        return carry

    lax.fori_loop(0, blocks // 2, far_blocks, 0)

    def place_of(block, slot):
        place = meta_ref[block, 2 + jnp.minimum(slot, slots - 1)]
        return jnp.where(slot < meta_ref[block, 0], place, leaves)

    def pair_places(block, slot):
        return place_of(block, slot), place_of(block, slot + 1)

    def pair_lefts(block, places):
        tile = point_tile(block)
        return [left_side(tile, middles[place]) for place in places]

    def advance(block, slot):
        ends = slot + 2 >= meta_ref[block, 0]
        later = jnp.where(ends, jnp.minimum(block + 1, blocks - 1), block)
        return later, jnp.where(ends, 0, slot + 2)

    def count_steps(block, total):
        return total + (meta_ref[block, 0] + 1) // 2

    steps = lax.fori_loop(0, blocks, count_steps, 0)
    block0, slot0 = 0, 0
    places0 = pair_places(block0, slot0)
    block1, slot1 = advance(block0, slot0)
    places1 = pair_places(block1, slot1)
    block2, slot2 = advance(block1, slot1)
    places2 = pair_places(block2, slot2)
    first = pair_lefts(block0, places0)
    for k in range(2):
        ready[k] = squares(first[k], rights[places0[k]])
    lefts[0], lefts[1] = pair_lefts(block1, places1)

    def near_step(step, carry):
        block, places, block1, places1, block2, places2, slot2 = carry
        coming = pair_lefts(block2, places2)
        found = [squares(lefts[k], rights[places1[k]]) for k in range(2)]
        block3, slot3 = advance(block2, slot2)
        places3 = pair_places(block3, slot3)
        shifts = [
            [
                [
                    jnp.broadcast_to(nodes[place, 3 + axis : 4 + axis, half * LANES : (half + 1) * LANES], (8, LANES))
                    for axis in range(3)
                ]
                for half in range(halves)
            ]
            for place in places
        ]
        for part in range(LANES // 8):
            rows = slice(part * 8, part * 8 + 8)
            total = [None] * 4
            for k in range(2):
                for half in range(halves):
                    inverse = 1.0 / ready[k, rows, half * LANES : (half + 1) * LANES]
                    weight = inverse * inverse
                    terms = [weight * shifts[k][half][axis] for axis in range(3)] + [weight]
                    total = [term if t is None else t + term for t, term in zip(total, terms)]
            for index in range(4):
                acc[block, index, rows] = acc[block, index, rows] + total[index]
        ready[0], ready[1] = found
        lefts[0], lefts[1] = coming
        return block1, places1, block2, places2, block3, places3, slot3

    lax.fori_loop(0, steps, near_step, (block0, places0, block1, places1, block2, places2, slot2))

    def finish(step, carry):
        for k in range(2):
            block = step * 2 + k
            sums = [
                jnp.sum(jnp.transpose(acc[block, index]), axis=0, keepdims=True) for index in range(4)
            ]
            moved_by = jnp.concatenate(sums[:3], axis=0) / sums[3]
            lanes = pl.ds(pl.multiple_of(block * LANES, LANES), LANES)
            start = pl.multiple_of((rank_ref[0] * blocks + block) * LANES, LANES)
            disp_ref[:, lanes] = moved_by
            moved_ref[:, lanes] = volume_ref[:, pl.ds(start, LANES)] + moved_by
        return carry

    lax.fori_loop(0, blocks // 2, finish, 0)


def cross(a, b):
    return (a[1] * b[2] - a[2] * b[1], a[2] * b[0] - a[0] * b[2], a[0] * b[1] - a[1] * b[0])


def dot(a, b):
    return a[0] * b[0] + a[1] * b[1] + a[2] * b[2]


FUNCS = 7


def wall_kernel(
    leaf_dev, halves, chunks, meta_ref, rank_ref, low_ref, high_ref, moved_ref, flags_ref, wall_ref,
    table, spheres, lefts, nearest, right_even, right_odd, ready_even, ready_odd,
    active, active_scalars, work, sem,
):
    half_dev = low_ref.shape[0]
    rows = leaf_dev * chunks
    blocks = wall_ref.shape[0]
    slots = meta_ref.shape[1] - 2
    base = leaf_dev * halves * 8
    lane_ids = lax.broadcasted_iota(jnp.int32, (rows, LANES), 1)

    def load_device(dev, src_ref, offset):
        place = dev + offset
        moved = []
        for axis in range(3):
            parts = []
            for half in range(halves):
                pieces = []
                for leaf in range(leaf_dev):
                    row = (leaf * halves + half) * 8
                    line = src_ref[dev, row + axis : row + axis + 1, :]
                    line = line + src_ref[dev, row + 3 + axis : row + 4 + axis, :]
                    pieces.append(jnp.broadcast_to(line, (chunks, LANES)))
                parts.append(jnp.concatenate(pieces, axis=0))
            moved.append(parts)
        corners = []
        for corner in range(3):
            ids = src_ref[dev, base + corner * rows : base + (corner + 1) * rows, :].astype(jnp.int32)
            lane = ids & (LANES - 1)
            vertex = []
            for axis in range(3):
                value = jnp.take_along_axis(moved[axis][0], lane, axis=1)
                for half in range(1, halves):
                    other = jnp.take_along_axis(moved[axis][half], lane, axis=1)
                    value = jnp.where(ids >= half * LANES, other, value)
                vertex.append(value)
            corners.append(vertex)
        a, b, c = corners
        ab = [b[k] - a[k] for k in range(3)]
        bc = [c[k] - b[k] for k in range(3)]
        ac = [c[k] - a[k] for k in range(3)]
        normal = cross(ab, ac)
        scale = 1.0 / jnp.sqrt(dot(normal, normal))
        normal = [v * scale for v in normal]
        tangents, insides, lengths = [], [], []
        for edge, sign in ((ab, 1.0), (bc, 1.0), (ac, -1.0)):
            length = jnp.sqrt(dot(edge, edge))
            scale = 1.0 / length
            along = [v * scale for v in edge]
            inside = cross(normal, along) if sign > 0 else cross(along, normal)
            tangents.append(along)
            insides.append(inside)
            lengths.append(0.5 * length)
        functions = [
            list(tangents[0]) + [-dot(a, tangents[0]) - lengths[0]],
            list(insides[0]) + [-dot(a, insides[0])],
            list(normal) + [-dot(a, normal)],
            list(tangents[1]) + [-dot(b, tangents[1]) - lengths[1]],
            list(insides[1]) + [-dot(b, insides[1])],
            list(tangents[2]) + [-dot(a, tangents[2]) - lengths[2]],
            list(insides[2]) + [-dot(a, insides[2])],
        ]
        values = [value for function in functions for value in function] + lengths
        for index, value in enumerate(values):
            table[pl.ds(pl.multiple_of((place * 32 + index) * rows, 8), rows), :] = value
        low = [jnp.min(jnp.minimum(jnp.minimum(a[k], b[k]), c[k]), axis=1, keepdims=True) for k in range(3)]
        high = [jnp.max(jnp.maximum(jnp.maximum(a[k], b[k]), c[k]), axis=1, keepdims=True) for k in range(3)]
        center = [0.5 * (low[k] + high[k]) for k in range(3)]
        squares = []
        for vertex in corners:
            diff = [vertex[k] - center[k] for k in range(3)]
            squares.append(dot(diff, diff))
        far = jnp.max(jnp.maximum(jnp.maximum(squares[0], squares[1]), squares[2]), axis=1, keepdims=True)
        close = jnp.min(jnp.minimum(jnp.minimum(squares[0], squares[1]), squares[2]), axis=1, keepdims=True)
        sphere = jnp.zeros((rows, LANES), jnp.float32)
        for index, value in enumerate(center + [jnp.sqrt(far), jnp.sqrt(close)]):
            sphere = jnp.where(lane_ids == index, value, sphere)
        spheres[pl.ds(pl.multiple_of(place * rows, rows), rows), :] = sphere

    def load_low(dev, carry):
        load_device(dev, low_ref, 0)
        return carry

    def load_high(dev, carry):
        load_device(dev, high_ref, half_dev)
        return carry

    lax.fori_loop(0, half_dev, load_low, 0, unroll=2)
    lax.fori_loop(0, half_dev, load_high, 0, unroll=2)

    dense_rows = slots * chunks
    dense_lane = lax.broadcasted_iota(jnp.int32, (dense_rows, LANES), 1)
    dense_slot = lax.broadcasted_iota(jnp.int32, (dense_rows, LANES), 0) // chunks

    def find_active(block, found):
        start = pl.multiple_of(block * LANES, LANES)
        here = moved_ref[:, pl.ds(start, LANES)]
        flags = flags_ref[pl.ds(rank_ref[0] * blocks + block, 1), :]
        half = jnp.concatenate([here, jnp.ones((1, LANES), jnp.float32)], axis=0)
        left = stack6(parts3(jnp.concatenate([half, half], axis=0)), LEFT)
        lefts[block] = jnp.transpose(left).astype(jnp.bfloat16)
        nearest[block] = jnp.full((LANES, LANES), big_value, jnp.float32)
        pieces = []
        for slot in range(slots):
            place = jnp.maximum(meta_ref[block, 2 + slot], 0)
            pieces.append(spheres[pl.ds(place * chunks, chunks), :])
        tile = jnp.concatenate(pieces, axis=0)
        cx, cy, cz, radius, close = (tile[:, k : k + 1] for k in range(5))
        dx, dy, dz = cx - here[0:1], cy - here[1:2], cz - here[2:3]
        distance = jnp.sqrt(dx * dx + dy * dy + dz * dz)
        real = dense_slot < meta_ref[block, 0]
        upper = jnp.min(jnp.where(real, distance + close, big_value), axis=0, keepdims=True)
        limit = jnp.where(flags == 1, upper * 1.0001 + 1e-4, -big_value)
        keep = jnp.where(real & (distance - radius <= limit), 1.0, 0.0)
        return jnp.where(dense_lane == block, jnp.max(keep, axis=1, keepdims=True), found)

    found = jnp.zeros((dense_rows, LANES), jnp.float32)
    active[...] = lax.fori_loop(0, blocks, find_active, found, unroll=2).astype(jnp.int32)
    copy = pltpu.make_async_copy(active, active_scalars, sem)
    copy.start()
    copy.wait()

    scale = 1 << (blocks - 1).bit_length()

    def list_block(block, items):
        def list_leaf(slot, items):
            code = meta_ref[block, 2 + slot] * (chunks * scale) + block
            for chunk in range(chunks):
                work[items] = code + chunk * scale
                items = items + active_scalars[slot * chunks + chunk, block]
            return items

        count = jnp.where(meta_ref[block, 1] > 0, meta_ref[block, 0], 0)
        return lax.fori_loop(0, count, list_leaf, items)

    items = lax.fori_loop(0, blocks, list_block, 0)
    upper_rows = lax.broadcasted_iota(jnp.int32, (8, LANES), 0) < 4

    def right_side(column):
        tiles = []
        for pair in range((FUNCS + 1) // 2):
            start = column // rows * (32 * rows) + column % rows + pair * 8 * rows
            parts = parts3(table[pl.ds(start, 8, stride=rows), :])
            for index in range(2):
                if pair * 2 + index < FUNCS:
                    mine = upper_rows if index == 0 else jnp.logical_not(upper_rows)
                    own = [jnp.where(mine, part, 0.0) for part in parts]
                    tiles.append(stack6(own, RIGHT))
        return jnp.concatenate(tiles, axis=1).astype(jnp.bfloat16)

    def products(block, right):
        return jnp.dot(lefts[block], right, preferred_element_type=jnp.float32)

    def evaluate(item, source):
        code = work[item]
        block, column = code % scale, code // scale
        start = column // rows * (32 * rows) + column % rows
        half_a, half_b, half_c = (
            jnp.broadcast_to(table[pl.ds(start + (28 + k) * rows, 1), :], (8, LANES)) for k in range(3)
        )
        for part in range(LANES // 8):
            here = slice(part * 8, part * 8 + 8)
            ta, sa, h, tb, sb, tc, sc = (
                source[here, k * LANES : (k + 1) * LANES] for k in range(FUNCS)
            )
            over_a = jnp.maximum(jnp.abs(ta) - half_a, 0.0)
            over_b = jnp.maximum(jnp.abs(tb) - half_b, 0.0)
            over_c = jnp.maximum(jnp.abs(tc) - half_c, 0.0)
            edge = jnp.minimum(sa * sa + over_a * over_a, sb * sb + over_b * over_b)
            edge = jnp.minimum(edge, sc * sc + over_c * over_c)
            inside = jnp.minimum(jnp.minimum(sa, sb), sc) >= 0.0
            square = jnp.where(inside, 0.0, edge) + h * h
            nearest[block, here] = jnp.minimum(nearest[block, here], square)

    @pl.when(items > 0)
    def _():
        for extra in range(4):
            work[items + extra] = work[items - 1]
        ready_even[...] = products(work[0] % scale, right_side(work[0] // scale))
        right_odd[...] = right_side(work[1] // scale)
        right_even[...] = right_side(work[2] // scale)

        def two_items(step, carry):
            item = step * 2
            ready_odd[...] = products(work[item + 1] % scale, right_odd[...])
            evaluate(item, ready_even)
            right_odd[...] = right_side(work[item + 3] // scale)
            ready_even[...] = products(work[item + 2] % scale, right_even[...])
            evaluate(item + 1, ready_odd)
            right_even[...] = right_side(work[item + 4] // scale)
            return carry

        lax.fori_loop(0, (items + 1) // 2, two_items, 0)

    def finish(block, carry):
        square = jnp.min(jnp.transpose(nearest[block]), axis=0, keepdims=True)
        flags = flags_ref[pl.ds(rank_ref[0] * blocks + block, 1), :]
        wall_ref[pl.ds(block, 1), :] = jnp.where(flags == 1, jnp.sqrt(square), 0.0)
        return carry

    lax.fori_loop(0, blocks, finish, 0, unroll=2)


def gather_order(vol_count, surf_count):
    steps = []
    bit = surf_count // 2
    while bit >= 1:
        steps.append(("surf", bit))
        bit //= 2
    bit = vol_count // 2
    while bit >= 1:
        steps.append(("vol", bit))
        bit //= 2
    return steps


def body(surface_points, surface_shift, facet_nodes, volume_points, near_wall, candidates):
    surf_count, vol_count = lax.axis_size("surf"), lax.axis_size("vol")
    sizes = {"surf": surf_count, "vol": vol_count}
    ranks = {"surf": lax.axis_index("surf"), "vol": lax.axis_index("vol")}
    leaf_dev, _, facet_len = facet_nodes.shape
    leaf_len = surface_points.shape[1] // leaf_dev
    halves, chunks = leaf_len // LANES, facet_len // LANES
    devices = surf_count * vol_count
    leaves = devices * leaf_dev
    slots = candidates.shape[1]
    blocks = candidates.shape[0] // surf_count
    share_len = volume_points.shape[1] // surf_count
    rows = leaf_dev * chunks
    payload_rows = leaf_dev * halves * 8 + 3 * rows
    vmem = pl.BlockSpec(memory_space=pltpu.VMEM)
    smem = pl.BlockSpec(memory_space=pltpu.SMEM)
    params = pltpu.CompilerParams(vmem_limit_bytes=60 * 1024 * 1024)

    held = pl.pallas_call(
        prep_kernel,
        out_shape=jax.ShapeDtypeStruct((1, payload_rows, LANES), jnp.float32),
        in_specs=[vmem] * 3,
        out_specs=vmem,
    )(surface_points, surface_shift, facet_nodes)
    steps = gather_order(vol_count, surf_count)
    for index, (axis, bit) in enumerate(steps):
        pairs = [(source, source ^ bit) for source in range(sizes[axis])]
        arrived = lax.ppermute(held, axis, pairs)
        if index < len(steps) - 1:
            held = jnp.concatenate([held, arrived], axis=0)

    own = lax.dynamic_slice_in_dim(candidates, ranks["surf"] * blocks, blocks, 0)
    owner = jnp.maximum(own, 0) // leaf_dev
    apart = {"surf": (owner % surf_count) ^ ranks["surf"], "vol": (owner // surf_count) ^ ranks["vol"]}
    place = jnp.zeros_like(own)
    for index, (axis, bit) in enumerate(steps):
        place = place + jnp.where((apart[axis] & bit) != 0, 1 << index, 0)
    place = place * leaf_dev + jnp.maximum(own, 0) % leaf_dev
    count = jnp.sum((own >= 0).astype(jnp.int32), axis=1, keepdims=True)
    flag_rows = near_wall.reshape(-1, LANES)
    own_flags = lax.dynamic_slice_in_dim(flag_rows, ranks["surf"] * blocks, blocks, 0)
    near = jnp.max(own_flags, axis=1, keepdims=True)
    place = jnp.where(own >= 0, place, -1)
    meta = jnp.concatenate([count, near, place], axis=1)
    rank = ranks["surf"].reshape(1).astype(jnp.int32)

    groups = -(-leaves // LANES)
    disp, moved = pl.pallas_call(
        functools.partial(near_kernel, leaf_dev, halves),
        out_shape=[jax.ShapeDtypeStruct((3, share_len), jnp.float32)] * 2,
        in_specs=[smem, smem, vmem, vmem, vmem],
        out_specs=[vmem, vmem],
        scratch_shapes=[
            pltpu.VMEM((leaves + 1, 8, leaf_len), jnp.float32),
            pltpu.VMEM((leaves + 1, 48, leaf_len), jnp.bfloat16),
            pltpu.VMEM((leaves + 1, 8, LANES), jnp.float32),
            pltpu.VMEM((8, groups * LANES), jnp.float32),
            pltpu.VMEM((blocks, 4, LANES, LANES), jnp.float32),
            pltpu.VMEM((2, LANES, leaf_len), jnp.float32),
            pltpu.VMEM((2, LANES, 48), jnp.bfloat16),
        ],
        compiler_params=params,
    )(meta, rank, held, arrived, volume_points)
    wall = pl.pallas_call(
        functools.partial(wall_kernel, leaf_dev, halves, chunks),
        out_shape=jax.ShapeDtypeStruct((blocks, LANES), jnp.float32),
        in_specs=[smem, smem, vmem, vmem, vmem, vmem],
        out_specs=vmem,
        scratch_shapes=[
            pltpu.VMEM((devices * rows * 32, LANES), jnp.float32),
            pltpu.VMEM((devices * rows, LANES), jnp.float32),
            pltpu.VMEM((blocks, LANES, 48), jnp.bfloat16),
            pltpu.VMEM((blocks, LANES, LANES), jnp.float32),
            pltpu.VMEM((48, FUNCS * LANES), jnp.bfloat16),
            pltpu.VMEM((48, FUNCS * LANES), jnp.bfloat16),
            pltpu.VMEM((LANES, FUNCS * LANES), jnp.float32),
            pltpu.VMEM((LANES, FUNCS * LANES), jnp.float32),
            pltpu.VMEM((slots * chunks, LANES), jnp.int32),
            pltpu.SMEM((slots * chunks, LANES), jnp.int32),
            pltpu.SMEM((blocks * slots * chunks + 8,), jnp.int32),
            pltpu.SemaphoreType.DMA,
        ],
        compiler_params=params,
    )(meta, rank, held, arrived, moved, flag_rows)
    return (disp, wall.reshape(-1))


def solution(mesh):
    placed = (
        P(None, ("vol", "surf")),
        P(None, ("vol", "surf")),
        P(("vol", "surf"), None, None),
        P(None, "vol"),
        P("vol"),
        P("vol", None),
    )
    return jax.shard_map(
        body,
        mesh=mesh,
        in_specs=placed,
        out_specs=(P(None, ("vol", "surf")), P(("vol", "surf"))),
        check_vma=False,
    )
```

```python
import functools

import jax
import jax.numpy as jnp
from jax import lax
from jax.experimental import pallas as pl
from jax.experimental.pallas import tpu as pltpu
from jax.sharding import PartitionSpec as P

smoothing = 0.01
big_value = 1e30
LANES = 128
COEFS = 24


def divide(value, by):
    if by & (by - 1) == 0:
        return lax.shift_right_logical(value, jnp.full_like(value, by.bit_length() - 1))
    return lax.div(value, jnp.full_like(value, by))


def prep_kernel(steps, surf_count, points_ref, shift_ref, facets_ref, near_ref, candidates_ref, out_ref, meta_ref, turned):
    corners, leaf_dev, facet_len = facets_ref.shape
    leaf_len = points_ref.shape[1] // leaf_dev
    halves, chunks = leaf_len // LANES, facet_len // LANES
    tail = jnp.where(lax.broadcasted_iota(jnp.int32, (2, LANES), 0) == 0, 1.0, 0.0)
    for leaf in range(leaf_dev):
        for half in range(halves):
            row = (leaf * halves + half) * 8
            lanes = pl.ds((leaf * halves + half) * LANES, LANES)
            out_ref[0, row : row + 3, :] = points_ref[:, lanes]
            out_ref[0, row + 3 : row + 6, :] = shift_ref[:, lanes]
            out_ref[0, row + 6 : row + 8, :] = tail
    base = leaf_dev * halves * 8
    for corner in range(corners):
        ids = facets_ref[corner].astype(jnp.float32)
        for leaf in range(leaf_dev):
            for chunk in range(chunks):
                row = base + (corner * leaf_dev + leaf) * chunks + chunk
                out_ref[0, row : row + 1, :] = ids[leaf : leaf + 1, chunk * LANES : (chunk + 1) * LANES]
    blocks, slots = meta_ref.shape[0], candidates_ref.shape[0]
    turned[...] = jnp.transpose(candidates_ref[...])
    ranks = {"surf": lax.axis_index("surf"), "vol": lax.axis_index("vol")}
    rows = pl.ds(ranks["surf"] * blocks, blocks)
    own = turned[rows, :]
    real = own >= 0
    safe = jnp.maximum(own, 0)
    owner = divide(safe, leaf_dev)
    vol = divide(owner, surf_count)
    apart = {"surf": (owner - vol * surf_count) ^ ranks["surf"], "vol": vol ^ ranks["vol"]}
    place = jnp.zeros_like(own)
    for index, (axis, bit) in enumerate(steps):
        place = place + jnp.where((apart[axis] & bit) != 0, 1 << index, 0)
    place = place * leaf_dev + (safe - owner * leaf_dev)
    meta_ref[:, 0:slots] = jnp.where(real, place, -1)
    count = jnp.sum(jnp.where(real, 1.0, 0.0), axis=1, keepdims=True)
    meta_ref[:, slots : slots + 1] = count.astype(jnp.int32)
    near = jnp.max(near_ref[rows, :].astype(jnp.float32), axis=1, keepdims=True)
    meta_ref[:, slots + 1 : slots + 2] = near.astype(jnp.int32)


def split3(value):
    first = value.astype(jnp.bfloat16)
    rest = value - first.astype(jnp.float32)
    second = rest.astype(jnp.bfloat16)
    third = (rest - second.astype(jnp.float32)).astype(jnp.bfloat16)
    return first, second, third


def stack6(tiles, order):
    return jnp.concatenate([tiles[k] for k in order], axis=0)


def parts3(tile):
    return [part.astype(jnp.float32) for part in split3(tile)]


NEAR_TOGETHER = 2
NEAR_STEPS = 3
LEFT = (0, 0, 0, 1, 1, 2)
RIGHT = (0, 1, 2, 0, 1, 0)


def near_kernel(
    leaf_dev, halves, meta_ref, low_ref, high_ref, volume_ref, disp_ref, moved_ref,
    nodes, rights, middles, moments, acc, ready, lefts, near_work,
):
    half_dev = low_ref.shape[0]
    leaves = nodes.shape[0] - 1
    blocks = disp_ref.shape[1] // LANES
    leaf_len = halves * LANES
    slots = meta_ref.shape[1] - 2
    lane_ids = lax.broadcasted_iota(jnp.int32, (8, LANES), 1)
    row_ids = lax.broadcasted_iota(jnp.int32, (8, LANES), 0)
    groups = moments.shape[1] // LANES

    def right_side(tile, center):
        rows = lax.broadcasted_iota(jnp.int32, tile.shape, 0)
        apart = jnp.where(rows < 3, tile - center, 0.0)
        norm = jnp.sum(apart * apart, axis=0, keepdims=True) + smoothing
        right = jnp.where(rows == 3, 1.0, jnp.where(rows == 4, norm, -2.0 * apart))
        return stack6(parts3(right), RIGHT).astype(jnp.bfloat16)

    def left_side(tile, center):
        offset = jnp.where(row_ids < 3, tile - center, 0.0)
        norm = jnp.sum(offset * offset, axis=0, keepdims=True)
        left = jnp.where(row_ids == 3, norm, jnp.where(row_ids == 4, 1.0, offset))
        return jnp.transpose(stack6(parts3(left), LEFT)).astype(jnp.bfloat16)

    def squares(left, right):
        return jnp.dot(left, right, preferred_element_type=jnp.float32)

    def point_tile(block):
        start = pl.multiple_of((lax.axis_index("surf") * blocks + block) * LANES, LANES)
        here = volume_ref[:, pl.ds(start, LANES)]
        return jnp.concatenate([here, jnp.zeros((5, LANES), jnp.float32)], axis=0)

    moments[...] = jnp.zeros_like(moments)
    nodes[leaves] = jnp.zeros_like(nodes[leaves])
    middles[leaves] = jnp.zeros_like(middles[leaves])
    away = lax.broadcasted_iota(jnp.int32, (48, leaf_len), 0) == 4
    rights[leaves] = jnp.where(away, 1e25, 0.0).astype(jnp.bfloat16)

    def load_device(dev, src_ref, offset):
        for leaf in range(leaf_dev):
            place = (dev + offset) * leaf_dev + leaf
            tiles = []
            for half in range(halves):
                row = (leaf * halves + half) * 8
                tiles.append(src_ref[dev, row : row + 8, :])
            whole = jnp.concatenate(tiles, axis=1)
            nodes[place] = whole
            total = functools.reduce(lambda a, b: a + b, tiles)
            total = jnp.sum(total, axis=1, keepdims=True)
            center = total * (1.0 / leaf_len)
            middles[place] = jnp.broadcast_to(center, (8, LANES))
            rights[place] = right_side(whole, center)
            group = place // LANES
            lanes = pl.ds(pl.multiple_of(group * LANES, LANES), LANES)
            moments[:, lanes] = jnp.where(
                lane_ids == place - group * LANES, total, moments[:, lanes]
            )

    leaf_bits = leaves.bit_length()
    each = -(-blocks // half_dev)

    def list_block(block, items):
        inside = jnp.minimum(block, blocks - 1)
        count = jnp.where(block < blocks, meta_ref[inside, slots], 0)
        for first in range(0, slots, NEAR_TOGETHER):
            code = inside << (NEAR_TOGETHER * leaf_bits)
            for k in range(NEAR_TOGETHER):
                slot = min(first + k, slots - 1)
                place = jnp.where(first + k < count, meta_ref[inside, slot], leaves)
                code = code | (place << (k * leaf_bits))
            near_work[items] = code
            items = items + jnp.where(first < count, 1, 0)
        return items

    def load_low(dev, items):
        load_device(dev, low_ref, 0)
        for k in range(each):
            items = list_block(dev * each + k, items)
        return items

    def load_high(dev, carry):
        load_device(dev, high_ref, half_dev)
        return carry

    items = lax.fori_loop(0, half_dev, load_low, 0, unroll=4)
    lax.fori_loop(0, half_dev, load_high, 0, unroll=4)

    def far_blocks(step, carry):
        here = [step * 2 + k for k in range(2)]
        centers, lefts = [], []
        for block in here:
            tile = point_tile(block)
            center = jnp.sum(tile, axis=1, keepdims=True) * (1.0 / LANES)
            centers.append(center)
            lefts.append(left_side(tile, center))
        for group in range(groups):
            tile = moments[:, group * LANES : (group + 1) * LANES]
            place = lane_ids[:1] + group * LANES
            found = [
                squares(lefts[k], right_side(tile * (1.0 / leaf_len), centers[k])) for k in range(2)
            ]
            for k in range(2):
                listed = place >= leaves
                for slot in range(slots):
                    listed = listed | (place == meta_ref[here[k], slot])
                mask = jnp.where(listed, 0.0, 1.0)
                inverse = 1.0 / found[k]
                weight = inverse * inverse * mask
                for index in range(4):
                    term = weight * tile[3 + index : 4 + index]
                    if group > 0:
                        term = term + acc[here[k], index]
                    acc[here[k], index] = term
        return carry

    lax.fori_loop(0, blocks // 2, far_blocks, 0)

    def step_at(item):
        code = near_work[item]
        mask = (1 << leaf_bits) - 1
        places = tuple(
            lax.shift_right_logical(code, k * leaf_bits) & mask for k in range(NEAR_TOGETHER)
        )
        return lax.shift_right_logical(code, NEAR_TOGETHER * leaf_bits), places

    def pair_lefts(block, places):
        tile = point_tile(block)
        return [left_side(tile, middles[place]) for place in places]

    for extra in range(3 * NEAR_STEPS):
        near_work[items + extra] = sum(leaves << (k * leaf_bits) for k in range(NEAR_TOGETHER))
    states = [step_at(k) for k in range(2 * NEAR_STEPS)]
    for k in range(NEAR_STEPS):
        first = pair_lefts(*states[k])
        coming = pair_lefts(*states[NEAR_STEPS + k])
        for leaf in range(NEAR_TOGETHER):
            ready[k, leaf] = squares(first[leaf], rights[states[k][1][leaf]])
            lefts[k, leaf] = coming[leaf]

    def near_steps(step, carry):
        states = [step_at(step * NEAR_STEPS + k) for k in range(3 * NEAR_STEPS)]
        for k in range(NEAR_STEPS):
            one_step(k, states)
        return carry

    def one_step(k, states):
        block, places = states[k]
        places1 = states[NEAR_STEPS + k][1]
        found = [squares(lefts[k, leaf], rights[places1[leaf]]) for leaf in range(NEAR_TOGETHER)]
        shifts = [
            [
                [
                    jnp.broadcast_to(nodes[place, 3 + axis : 4 + axis, half * LANES : (half + 1) * LANES], (8, LANES))
                    for axis in range(3)
                ]
                for half in range(halves)
            ]
            for place in places
        ]
        for part in range(LANES // 8):
            rows = slice(part * 8, part * 8 + 8)
            total = [None] * 4
            for leaf in range(NEAR_TOGETHER):
                for half in range(halves):
                    inverse = 1.0 / ready[k, leaf, rows, half * LANES : (half + 1) * LANES]
                    weight = inverse * inverse
                    terms = [weight * shifts[leaf][half][axis] for axis in range(3)] + [weight]
                    total = [term if t is None else t + term for t, term in zip(total, terms)]
            for index in range(4):
                acc[block, index, rows] = acc[block, index, rows] + total[index]
        coming = pair_lefts(*states[2 * NEAR_STEPS + k])
        for leaf in range(NEAR_TOGETHER):
            ready[k, leaf] = found[leaf]
            lefts[k, leaf] = coming[leaf]

    lax.fori_loop(0, lax.div(items + NEAR_STEPS - 1, NEAR_STEPS), near_steps, 0)

    def finish(step, carry):
        for k in range(2):
            block = step * 2 + k
            sums = [
                jnp.sum(jnp.transpose(acc[block, index]), axis=0, keepdims=True) for index in range(4)
            ]
            moved_by = jnp.concatenate(sums[:3], axis=0) / sums[3]
            lanes = pl.ds(pl.multiple_of(block * LANES, LANES), LANES)
            start = pl.multiple_of((lax.axis_index("surf") * blocks + block) * LANES, LANES)
            disp_ref[:, lanes] = moved_by
            moved_ref[:, lanes] = volume_ref[:, pl.ds(start, LANES)] + moved_by
        return carry

    lax.fori_loop(0, blocks // 2, finish, 0)


def cross(a, b):
    return (a[1] * b[2] - a[2] * b[1], a[2] * b[0] - a[0] * b[2], a[0] * b[1] - a[1] * b[0])


def dot(a, b):
    return a[0] * b[0] + a[1] * b[1] + a[2] * b[2]


FUNCS = 7
LIST_SLOTS = 4
TOGETHER = 6


def wall_kernel(
    leaf_dev, halves, chunks, meta_ref, low_ref, high_ref, moved_ref, flags_ref, wall_ref,
    table, spheres, lefts, nearest, rights, products_of,
    active, active_scalars, work, sem,
):
    half_dev = low_ref.shape[0]
    rows = leaf_dev * chunks
    blocks = wall_ref.shape[0]
    slots = meta_ref.shape[1] - 2
    base = leaf_dev * halves * 8
    lane_ids = lax.broadcasted_iota(jnp.int32, (rows, LANES), 1)

    def load_device(dev, src_ref, offset):
        place = dev + offset
        moved = []
        for axis in range(3):
            parts = []
            for half in range(halves):
                pieces = []
                for leaf in range(leaf_dev):
                    row = (leaf * halves + half) * 8
                    line = src_ref[dev, row + axis : row + axis + 1, :]
                    line = line + src_ref[dev, row + 3 + axis : row + 4 + axis, :]
                    pieces.append(jnp.broadcast_to(line, (chunks, LANES)))
                parts.append(jnp.concatenate(pieces, axis=0))
            moved.append(parts)
        corners = []
        for corner in range(3):
            ids = src_ref[dev, base + corner * rows : base + (corner + 1) * rows, :].astype(jnp.int32)
            lane = ids & (LANES - 1)
            vertex = []
            for axis in range(3):
                value = jnp.take_along_axis(moved[axis][0], lane, axis=1)
                for half in range(1, halves):
                    other = jnp.take_along_axis(moved[axis][half], lane, axis=1)
                    value = jnp.where(ids >= half * LANES, other, value)
                vertex.append(value)
            corners.append(vertex)
        a, b, c = corners
        ab = [b[k] - a[k] for k in range(3)]
        bc = [c[k] - b[k] for k in range(3)]
        ac = [c[k] - a[k] for k in range(3)]
        normal = cross(ab, ac)
        scale = 1.0 / jnp.sqrt(dot(normal, normal))
        normal = [v * scale for v in normal]
        tangents, insides, lengths = [], [], []
        for edge, sign in ((ab, 1.0), (bc, 1.0), (ac, -1.0)):
            length = jnp.sqrt(dot(edge, edge))
            scale = 1.0 / length
            along = [v * scale for v in edge]
            inside = cross(normal, along) if sign > 0 else cross(along, normal)
            tangents.append(along)
            insides.append(inside)
            lengths.append(0.5 * length)
        functions = [
            list(tangents[0]) + [-dot(a, tangents[0]) - lengths[0]],
            list(insides[0]) + [-dot(a, insides[0])],
            list(normal) + [-dot(a, normal)],
            list(tangents[1]) + [-dot(b, tangents[1]) - lengths[1]],
            list(insides[1]) + [-dot(b, insides[1])],
            list(tangents[2]) + [-dot(a, tangents[2]) - lengths[2]],
            list(insides[2]) + [-dot(a, insides[2])],
        ]
        values = [value for function in functions for value in function] + lengths
        for index, value in enumerate(values):
            table[pl.ds(pl.multiple_of((place * 32 + index) * rows, 8), rows), :] = value
        low = [jnp.min(jnp.minimum(jnp.minimum(a[k], b[k]), c[k]), axis=1, keepdims=True) for k in range(3)]
        high = [jnp.max(jnp.maximum(jnp.maximum(a[k], b[k]), c[k]), axis=1, keepdims=True) for k in range(3)]
        center = [0.5 * (low[k] + high[k]) for k in range(3)]
        squares = []
        for vertex in corners:
            diff = [vertex[k] - center[k] for k in range(3)]
            squares.append(dot(diff, diff))
        far = jnp.max(jnp.maximum(jnp.maximum(squares[0], squares[1]), squares[2]), axis=1, keepdims=True)
        close = jnp.min(jnp.minimum(jnp.minimum(squares[0], squares[1]), squares[2]), axis=1, keepdims=True)
        sphere = jnp.zeros((rows, LANES), jnp.float32)
        for index, value in enumerate(center + [jnp.sqrt(far), jnp.sqrt(close)]):
            sphere = jnp.where(lane_ids == index, value, sphere)
        spheres[pl.ds(pl.multiple_of(place * rows, rows), rows), :] = sphere

    def load_low(dev, carry):
        load_device(dev, low_ref, 0)
        return carry

    def load_high(dev, carry):
        load_device(dev, high_ref, half_dev)
        return carry

    lax.fori_loop(0, half_dev, load_low, 0, unroll=4)
    lax.fori_loop(0, half_dev, load_high, 0, unroll=4)

    dense_rows = slots * chunks
    dense_lane = lax.broadcasted_iota(jnp.int32, (dense_rows, LANES), 1)
    dense_slot = lax.broadcasted_iota(jnp.int32, (dense_rows, LANES), 0) // chunks

    def find_active(block, found):
        start = pl.multiple_of(block * LANES, LANES)
        here = moved_ref[:, pl.ds(start, LANES)]
        flags = flags_ref[pl.ds(lax.axis_index("surf") * blocks + block, 1), :]
        half = jnp.concatenate([here, jnp.ones((1, LANES), jnp.float32)], axis=0)
        left = stack6(parts3(jnp.concatenate([half, half], axis=0)), LEFT)
        lefts[block] = jnp.transpose(left).astype(jnp.bfloat16)
        nearest[block] = jnp.full((LANES, LANES), big_value, jnp.float32)
        pieces = []
        for slot in range(slots):
            place = jnp.maximum(meta_ref[block, slot], 0)
            pieces.append(spheres[pl.ds(place * chunks, chunks), :])
        tile = jnp.concatenate(pieces, axis=0)
        cx, cy, cz, radius, close = (tile[:, k : k + 1] for k in range(5))
        dx, dy, dz = cx - here[0:1], cy - here[1:2], cz - here[2:3]
        distance = jnp.sqrt(dx * dx + dy * dy + dz * dz)
        real = dense_slot < meta_ref[block, slots]
        upper = jnp.min(jnp.where(real, distance + close, big_value), axis=0, keepdims=True)
        limit = jnp.where(flags == 1, upper * 1.0001 + 1e-4, -big_value)
        keep = jnp.where(real & (distance - radius <= limit), 1.0, 0.0)
        return jnp.where(dense_lane == block, jnp.max(keep, axis=1, keepdims=True), found)

    found = jnp.zeros((dense_rows, LANES), jnp.float32)
    active[...] = lax.fori_loop(0, blocks, find_active, found, unroll=4).astype(jnp.int32)
    copy = pltpu.make_async_copy(active, active_scalars, sem)
    copy.start()
    copy.wait()

    shift = (blocks - 1).bit_length()
    scale = 1 << shift

    def list_block(block, items):
        def list_leaves(group, items):
            for k in range(LIST_SLOTS):
                slot = group * LIST_SLOTS + k
                place = jnp.maximum(meta_ref[block, jnp.minimum(slot, slots - 1)], 0)
                row = divide(place, leaf_dev) * (32 * rows - leaf_dev * chunks) + place * chunks
                code = (row << shift) + block
                for chunk in range(chunks):
                    work[items] = code + (chunk << shift)
                    items = items + active_scalars[slot * chunks + chunk, block]
            return items

        count = jnp.where(meta_ref[block, slots + 1] > 0, meta_ref[block, slots], 0)
        return lax.fori_loop(0, divide(count + LIST_SLOTS - 1, LIST_SLOTS), list_leaves, items)

    items = lax.fori_loop(0, blocks, list_block, 0)
    upper_rows = lax.broadcasted_iota(jnp.int32, (8, LANES), 0) < 4

    def split(code):
        return code & (scale - 1), lax.shift_right_logical(code, shift)

    def right_side(code):
        first = split(code)[1]
        tiles = []
        for pair in range((FUNCS + 1) // 2):
            parts = parts3(table[pl.ds(first + pair * 8 * rows, 8, stride=rows), :])
            for index in range(2):
                if pair * 2 + index < FUNCS:
                    mine = upper_rows if index == 0 else jnp.logical_not(upper_rows)
                    own = [jnp.where(mine, part, 0.0) for part in parts]
                    tiles.append(stack6(own, RIGHT))
        return jnp.concatenate(tiles, axis=1).astype(jnp.bfloat16)

    def products(block, right):
        return jnp.dot(lefts[block], right, preferred_element_type=jnp.float32)

    def evaluate(item, source):
        block, start = split(work[item])
        half_a, half_b, half_c = (
            jnp.broadcast_to(table[pl.ds(start + (28 + k) * rows, 1), :], (8, LANES)) for k in range(3)
        )
        for part in range(LANES // 8):
            here = slice(part * 8, part * 8 + 8)
            ta, sa, h, tb, sb, tc, sc = (
                source[here, k * LANES : (k + 1) * LANES] for k in range(FUNCS)
            )
            over_a = jnp.maximum(jnp.abs(ta) - half_a, 0.0)
            over_b = jnp.maximum(jnp.abs(tb) - half_b, 0.0)
            over_c = jnp.maximum(jnp.abs(tc) - half_c, 0.0)
            edge = jnp.minimum(sa * sa + over_a * over_a, sb * sb + over_b * over_b)
            edge = jnp.minimum(edge, sc * sc + over_c * over_c)
            inside = jnp.minimum(jnp.minimum(sa, sb), sc) >= 0.0
            square = jnp.where(inside, 0.0, edge) + h * h
            nearest[block, here] = jnp.minimum(nearest[block, here], square)

    @pl.when(items > 0)
    def _():
        for extra in range(3 * TOGETHER):
            work[items + extra] = work[items - 1]
        def product(code, right):
            return products(split(code)[0], right)

        for k in range(TOGETHER):
            products_of[k] = product(work[k], right_side(work[k]))
            rights[k] = right_side(work[TOGETHER + k])

        def some_items(step, carry):
            item = step * TOGETHER
            for k in range(TOGETHER):
                coming = product(work[item + TOGETHER + k], rights[k])
                evaluate(item + k, products_of.at[k])
                products_of[k] = coming
                rights[k] = right_side(work[item + 2 * TOGETHER + k])
            return carry

        lax.fori_loop(0, lax.div(items + TOGETHER - 1, TOGETHER), some_items, 0)

    def finish(block, carry):
        square = jnp.min(jnp.transpose(nearest[block]), axis=0, keepdims=True)
        flags = flags_ref[pl.ds(lax.axis_index("surf") * blocks + block, 1), :]
        wall_ref[pl.ds(block, 1), :] = jnp.where(flags == 1, jnp.sqrt(square), 0.0)
        return carry

    lax.fori_loop(0, blocks, finish, 0, unroll=2)


def gather_order(vol_count, surf_count):
    steps = []
    bit = surf_count // 2
    while bit >= 1:
        steps.append(("surf", bit))
        bit //= 2
    bit = vol_count // 2
    while bit >= 1:
        steps.append(("vol", bit))
        bit //= 2
    return steps


def body(surface_points, surface_shift, facet_nodes, volume_points, near_wall, candidates):
    surf_count, vol_count = lax.axis_size("surf"), lax.axis_size("vol")
    sizes = {"surf": surf_count, "vol": vol_count}
    leaf_dev, _, facet_len = facet_nodes.shape
    leaf_len = surface_points.shape[1] // leaf_dev
    halves, chunks = leaf_len // LANES, facet_len // LANES
    devices = surf_count * vol_count
    leaves = devices * leaf_dev
    slots = candidates.shape[1]
    blocks = candidates.shape[0] // surf_count
    share_len = volume_points.shape[1] // surf_count
    rows = leaf_dev * chunks
    payload_rows = leaf_dev * halves * 8 + 3 * rows
    vmem = pl.BlockSpec(memory_space=pltpu.VMEM)
    smem = pl.BlockSpec(memory_space=pltpu.SMEM)
    params = pltpu.CompilerParams(vmem_limit_bytes=60 * 1024 * 1024)

    flag_rows = near_wall.reshape(-1, LANES)
    steps = gather_order(vol_count, surf_count)
    held, meta = pl.pallas_call(
        functools.partial(prep_kernel, steps, surf_count),
        out_shape=[
            jax.ShapeDtypeStruct((1, payload_rows, LANES), jnp.float32),
            jax.ShapeDtypeStruct((blocks, slots + 2), jnp.int32),
        ],
        in_specs=[vmem] * 5,
        out_specs=[vmem] * 2,
        scratch_shapes=[pltpu.VMEM(candidates.shape, jnp.int32)],
    )(surface_points, surface_shift, jnp.transpose(facet_nodes, (1, 0, 2)), flag_rows, jnp.transpose(candidates))
    for index, (axis, bit) in enumerate(steps):
        pairs = [(source, source ^ bit) for source in range(sizes[axis])]
        arrived = lax.ppermute(held, axis, pairs)
        if index < len(steps) - 1:
            held = jnp.concatenate([held, arrived], axis=0)

    groups = -(-leaves // LANES)
    disp, moved = pl.pallas_call(
        functools.partial(near_kernel, leaf_dev, halves),
        out_shape=[jax.ShapeDtypeStruct((3, share_len), jnp.float32)] * 2,
        in_specs=[smem, vmem, vmem, vmem],
        out_specs=[vmem, vmem],
        scratch_shapes=[
            pltpu.VMEM((leaves + 1, 8, leaf_len), jnp.float32),
            pltpu.VMEM((leaves + 1, 48, leaf_len), jnp.bfloat16),
            pltpu.VMEM((leaves + 1, 8, LANES), jnp.float32),
            pltpu.VMEM((8, groups * LANES), jnp.float32),
            pltpu.VMEM((blocks, 4, LANES, LANES), jnp.float32),
            pltpu.VMEM((NEAR_STEPS, NEAR_TOGETHER, LANES, leaf_len), jnp.float32),
            pltpu.VMEM((NEAR_STEPS, NEAR_TOGETHER, LANES, 48), jnp.bfloat16),
            pltpu.SMEM((blocks * (slots // NEAR_TOGETHER + 1) + 3 * NEAR_STEPS,), jnp.int32),
        ],
        compiler_params=params,
    )(meta, held, arrived, volume_points)
    wall = pl.pallas_call(
        functools.partial(wall_kernel, leaf_dev, halves, chunks),
        out_shape=jax.ShapeDtypeStruct((blocks, LANES), jnp.float32),
        in_specs=[smem, vmem, vmem, vmem, vmem],
        out_specs=vmem,
        scratch_shapes=[
            pltpu.VMEM((devices * rows * 32, LANES), jnp.float32),
            pltpu.VMEM((devices * rows, LANES), jnp.float32),
            pltpu.VMEM((blocks, LANES, 48), jnp.bfloat16),
            pltpu.VMEM((blocks, LANES, LANES), jnp.float32),
            pltpu.VMEM((TOGETHER, 48, FUNCS * LANES), jnp.bfloat16),
            pltpu.VMEM((TOGETHER, LANES, FUNCS * LANES), jnp.float32),
            pltpu.VMEM((slots * chunks, LANES), jnp.int32),
            pltpu.SMEM((slots * chunks, LANES), jnp.int32),
            pltpu.SMEM((blocks * slots * chunks + 3 * TOGETHER,), jnp.int32),
            pltpu.SemaphoreType.DMA,
        ],
        compiler_params=params,
    )(meta, held, arrived, moved, flag_rows)
    return (disp, wall.reshape(-1))


def solution(mesh):
    placed = (
        P(None, ("vol", "surf")),
        P(None, ("vol", "surf")),
        P(("vol", "surf"), None, None),
        P(None, "vol"),
        P("vol"),
        P("vol", None),
    )
    return jax.shard_map(
        body,
        mesh=mesh,
        in_specs=placed,
        out_specs=(P(None, ("vol", "surf")), P(("vol", "surf"))),
        check_vma=False,
    )
```

```python
import functools

import jax
import jax.numpy as jnp
from jax import lax
from jax.experimental import pallas as pl
from jax.experimental.pallas import tpu as pltpu
from jax.sharding import PartitionSpec as P

smoothing = 0.01
big_value = 1e30
LANES = 128
COEFS = 24


def divide(value, by):
    if by & (by - 1) == 0:
        return lax.shift_right_logical(value, jnp.full_like(value, by.bit_length() - 1))
    return lax.div(value, jnp.full_like(value, by))


def prep_kernel(steps, surf_count, points_ref, shift_ref, facets_ref, near_ref, candidates_ref, out_ref, meta_ref, turned):
    corners, leaf_dev, facet_len = facets_ref.shape
    leaf_len = points_ref.shape[1] // leaf_dev
    halves, chunks = leaf_len // LANES, facet_len // LANES
    tail = jnp.where(lax.broadcasted_iota(jnp.int32, (2, LANES), 0) == 0, 1.0, 0.0)
    for leaf in range(leaf_dev):
        for half in range(halves):
            row = (leaf * halves + half) * 8
            lanes = pl.ds((leaf * halves + half) * LANES, LANES)
            out_ref[0, row : row + 3, :] = points_ref[:, lanes]
            out_ref[0, row + 3 : row + 6, :] = shift_ref[:, lanes]
            out_ref[0, row + 6 : row + 8, :] = tail
    base = leaf_dev * halves * 8
    for corner in range(corners):
        ids = facets_ref[corner].astype(jnp.float32)
        for leaf in range(leaf_dev):
            for chunk in range(chunks):
                row = base + (corner * leaf_dev + leaf) * chunks + chunk
                out_ref[0, row : row + 1, :] = ids[leaf : leaf + 1, chunk * LANES : (chunk + 1) * LANES]
    blocks, slots = meta_ref.shape[0], candidates_ref.shape[0]
    turned[...] = jnp.transpose(candidates_ref[...])
    ranks = {"surf": lax.axis_index("surf"), "vol": lax.axis_index("vol")}
    rows = pl.ds(ranks["surf"] * blocks, blocks)
    own = turned[rows, :]
    real = own >= 0
    safe = jnp.maximum(own, 0)
    owner = divide(safe, leaf_dev)
    vol = divide(owner, surf_count)
    apart = {"surf": (owner - vol * surf_count) ^ ranks["surf"], "vol": vol ^ ranks["vol"]}
    place = jnp.zeros_like(own)
    for index, (axis, bit) in enumerate(steps):
        place = place + jnp.where((apart[axis] & bit) != 0, 1 << index, 0)
    place = place * leaf_dev + (safe - owner * leaf_dev)
    meta_ref[:, 0:slots] = jnp.where(real, place, -1)
    count = jnp.sum(jnp.where(real, 1.0, 0.0), axis=1, keepdims=True)
    meta_ref[:, slots : slots + 1] = count.astype(jnp.int32)
    near = jnp.max(near_ref[rows, :].astype(jnp.float32), axis=1, keepdims=True)
    meta_ref[:, slots + 1 : slots + 2] = near.astype(jnp.int32)


def split3(value):
    first = value.astype(jnp.bfloat16)
    rest = value - first.astype(jnp.float32)
    second = rest.astype(jnp.bfloat16)
    third = (rest - second.astype(jnp.float32)).astype(jnp.bfloat16)
    return first, second, third


def stack6(tiles, order):
    return jnp.concatenate([tiles[k] for k in order], axis=0)


def parts3(tile):
    return [part.astype(jnp.float32) for part in split3(tile)]


NEAR_TOGETHER = 2
NEAR_STEPS = 3
LEFT = (0, 0, 0, 1, 1, 2)
RIGHT = (0, 1, 2, 0, 1, 0)


def near_kernel(
    leaf_dev, halves, meta_ref, low_ref, high_ref, volume_ref, disp_ref, moved_ref,
    nodes, rights, middles, moments, acc, ready, lefts, near_work,
):
    half_dev = low_ref.shape[0]
    leaves = nodes.shape[0] - 1
    blocks = disp_ref.shape[1] // LANES
    leaf_len = halves * LANES
    slots = meta_ref.shape[1] - 2
    lane_ids = lax.broadcasted_iota(jnp.int32, (8, LANES), 1)
    row_ids = lax.broadcasted_iota(jnp.int32, (8, LANES), 0)
    groups = moments.shape[1] // LANES

    def right_side(tile, center):
        rows = lax.broadcasted_iota(jnp.int32, tile.shape, 0)
        apart = jnp.where(rows < 3, tile - center, 0.0)
        norm = jnp.sum(apart * apart, axis=0, keepdims=True) + smoothing
        right = jnp.where(rows == 3, 1.0, jnp.where(rows == 4, norm, -2.0 * apart))
        return stack6(parts3(right), RIGHT).astype(jnp.bfloat16)

    def left_side(tile, center):
        offset = jnp.where(row_ids < 3, tile - center, 0.0)
        norm = jnp.sum(offset * offset, axis=0, keepdims=True)
        left = jnp.where(row_ids == 3, norm, jnp.where(row_ids == 4, 1.0, offset))
        return jnp.transpose(stack6(parts3(left), LEFT)).astype(jnp.bfloat16)

    def squares(left, right):
        return jnp.dot(left, right, preferred_element_type=jnp.float32)

    def point_tile(block):
        start = pl.multiple_of((lax.axis_index("surf") * blocks + block) * LANES, LANES)
        here = volume_ref[:, pl.ds(start, LANES)]
        return jnp.concatenate([here, jnp.zeros((5, LANES), jnp.float32)], axis=0)

    moments[...] = jnp.zeros_like(moments)
    nodes[leaves] = jnp.zeros_like(nodes[leaves])
    middles[leaves] = jnp.zeros_like(middles[leaves])
    away = lax.broadcasted_iota(jnp.int32, (48, leaf_len), 0) == 4
    rights[leaves] = jnp.where(away, 1e25, 0.0).astype(jnp.bfloat16)

    def load_device(dev, src_ref, offset):
        for leaf in range(leaf_dev):
            place = (dev + offset) * leaf_dev + leaf
            tiles = []
            for half in range(halves):
                row = (leaf * halves + half) * 8
                tiles.append(src_ref[dev, row : row + 8, :])
            whole = jnp.concatenate(tiles, axis=1)
            nodes[place] = whole
            total = functools.reduce(lambda a, b: a + b, tiles)
            total = jnp.sum(total, axis=1, keepdims=True)
            center = total * (1.0 / leaf_len)
            middles[place] = jnp.broadcast_to(center, (8, LANES))
            rights[place] = right_side(whole, center)
            group = place // LANES
            lanes = pl.ds(pl.multiple_of(group * LANES, LANES), LANES)
            moments[:, lanes] = jnp.where(
                lane_ids == place - group * LANES, total, moments[:, lanes]
            )

    leaf_bits = leaves.bit_length()
    each = -(-blocks // half_dev)

    def list_block(block, items):
        inside = jnp.minimum(block, blocks - 1)
        count = jnp.where(block < blocks, meta_ref[inside, slots], 0)
        for first in range(0, slots, NEAR_TOGETHER):
            code = inside << (NEAR_TOGETHER * leaf_bits)
            for k in range(NEAR_TOGETHER):
                slot = min(first + k, slots - 1)
                place = jnp.where(first + k < count, meta_ref[inside, slot], leaves)
                code = code | (place << (k * leaf_bits))
            near_work[items] = code
            items = items + jnp.where(first < count, 1, 0)
        return items

    def load_low(dev, items):
        load_device(dev, low_ref, 0)
        for k in range(each):
            items = list_block(dev * each + k, items)
        return items

    def load_high(dev, carry):
        load_device(dev, high_ref, half_dev)
        return carry

    items = lax.fori_loop(0, half_dev, load_low, 0, unroll=4)
    lax.fori_loop(0, half_dev, load_high, 0, unroll=4)

    def far_blocks(step, carry):
        here = [step * 2 + k for k in range(2)]
        centers, lefts = [], []
        for block in here:
            tile = point_tile(block)
            center = jnp.sum(tile, axis=1, keepdims=True) * (1.0 / LANES)
            centers.append(center)
            lefts.append(left_side(tile, center))
        for group in range(groups):
            tile = moments[:, group * LANES : (group + 1) * LANES]
            place = lane_ids[:1] + group * LANES
            found = [
                squares(lefts[k], right_side(tile * (1.0 / leaf_len), centers[k])) for k in range(2)
            ]
            for k in range(2):
                listed = place >= leaves
                for slot in range(slots):
                    listed = listed | (place == meta_ref[here[k], slot])
                mask = jnp.where(listed, 0.0, 1.0)
                inverse = 1.0 / found[k]
                weight = inverse * inverse * mask
                for index in range(4):
                    term = weight * tile[3 + index : 4 + index]
                    if group > 0:
                        term = term + acc[here[k], index]
                    acc[here[k], index] = term
        return carry

    lax.fori_loop(0, blocks // 2, far_blocks, 0)

    def step_at(item):
        code = near_work[item]
        mask = (1 << leaf_bits) - 1
        places = tuple(
            lax.shift_right_logical(code, k * leaf_bits) & mask for k in range(NEAR_TOGETHER)
        )
        return lax.shift_right_logical(code, NEAR_TOGETHER * leaf_bits), places

    def pair_lefts(block, places):
        tile = point_tile(block)
        return [left_side(tile, middles[place]) for place in places]

    for extra in range(3 * NEAR_STEPS):
        near_work[items + extra] = sum(leaves << (k * leaf_bits) for k in range(NEAR_TOGETHER))
    states = [step_at(k) for k in range(2 * NEAR_STEPS)]
    for k in range(NEAR_STEPS):
        first = pair_lefts(*states[k])
        coming = pair_lefts(*states[NEAR_STEPS + k])
        for leaf in range(NEAR_TOGETHER):
            ready[k, leaf] = squares(first[leaf], rights[states[k][1][leaf]])
            lefts[k, leaf] = coming[leaf]

    def near_steps(step, carry):
        states = [step_at(step * NEAR_STEPS + k) for k in range(3 * NEAR_STEPS)]
        for k in range(NEAR_STEPS):
            one_step(k, states)
        return carry

    def one_step(k, states):
        block, places = states[k]
        places1 = states[NEAR_STEPS + k][1]
        found = [squares(lefts[k, leaf], rights[places1[leaf]]) for leaf in range(NEAR_TOGETHER)]
        shifts = [
            [
                [
                    jnp.broadcast_to(nodes[place, 3 + axis : 4 + axis, half * LANES : (half + 1) * LANES], (8, LANES))
                    for axis in range(3)
                ]
                for half in range(halves)
            ]
            for place in places
        ]
        for part in range(LANES // 8):
            rows = slice(part * 8, part * 8 + 8)
            total = [None] * 4
            for leaf in range(NEAR_TOGETHER):
                for half in range(halves):
                    inverse = 1.0 / ready[k, leaf, rows, half * LANES : (half + 1) * LANES]
                    weight = inverse * inverse
                    terms = [weight * shifts[leaf][half][axis] for axis in range(3)] + [weight]
                    total = [term if t is None else t + term for t, term in zip(total, terms)]
            for index in range(4):
                acc[block, index, rows] = acc[block, index, rows] + total[index]
        coming = pair_lefts(*states[2 * NEAR_STEPS + k])
        for leaf in range(NEAR_TOGETHER):
            ready[k, leaf] = found[leaf]
            lefts[k, leaf] = coming[leaf]

    lax.fori_loop(0, lax.div(items + NEAR_STEPS - 1, NEAR_STEPS), near_steps, 0)

    def finish(step, carry):
        for k in range(2):
            block = step * 2 + k
            sums = [
                jnp.sum(jnp.transpose(acc[block, index]), axis=0, keepdims=True) for index in range(4)
            ]
            moved_by = jnp.concatenate(sums[:3], axis=0) / sums[3]
            lanes = pl.ds(pl.multiple_of(block * LANES, LANES), LANES)
            start = pl.multiple_of((lax.axis_index("surf") * blocks + block) * LANES, LANES)
            disp_ref[:, lanes] = moved_by
            moved_ref[:, lanes] = volume_ref[:, pl.ds(start, LANES)] + moved_by
        return carry

    lax.fori_loop(0, blocks // 2, finish, 0)


def cross(a, b):
    return (a[1] * b[2] - a[2] * b[1], a[2] * b[0] - a[0] * b[2], a[0] * b[1] - a[1] * b[0])


def dot(a, b):
    return a[0] * b[0] + a[1] * b[1] + a[2] * b[2]


FUNCS = 7
LIST_SLOTS = 4
TOGETHER = 6


def wall_kernel(
    leaf_dev, halves, chunks, meta_ref, low_ref, high_ref, low_ids, high_ids, moved_ref, flags_ref, wall_ref,
    table, spheres, lefts, nearest, rights, products_of,
    active, active_scalars, work, sem,
):
    half_dev = low_ref.shape[0]
    rows = leaf_dev * chunks
    blocks = wall_ref.shape[0]
    slots = meta_ref.shape[1] - 2
    lane_ids = lax.broadcasted_iota(jnp.int32, (rows, LANES), 1)

    def load_device(dev, src_ref, ids_ref, offset):
        place = dev + offset
        moved = []
        for axis in range(3):
            parts = []
            for half in range(halves):
                pieces = []
                for leaf in range(leaf_dev):
                    row = (leaf * halves + half) * 8
                    line = src_ref[dev, row + axis : row + axis + 1, :]
                    line = line + src_ref[dev, row + 3 + axis : row + 4 + axis, :]
                    pieces.append(jnp.broadcast_to(line, (chunks, LANES)))
                parts.append(jnp.concatenate(pieces, axis=0))
            moved.append(parts)
        corners = []
        for corner in range(3):
            ids = ids_ref[dev, corner * rows : (corner + 1) * rows, :].astype(jnp.int32)
            lane = ids & (LANES - 1)
            vertex = []
            for axis in range(3):
                value = jnp.take_along_axis(moved[axis][0], lane, axis=1)
                for half in range(1, halves):
                    other = jnp.take_along_axis(moved[axis][half], lane, axis=1)
                    value = jnp.where(ids >= half * LANES, other, value)
                vertex.append(value)
            corners.append(vertex)
        a, b, c = corners
        ab = [b[k] - a[k] for k in range(3)]
        bc = [c[k] - b[k] for k in range(3)]
        ac = [c[k] - a[k] for k in range(3)]
        normal = cross(ab, ac)
        scale = 1.0 / jnp.sqrt(dot(normal, normal))
        normal = [v * scale for v in normal]
        tangents, insides, lengths = [], [], []
        for edge, sign in ((ab, 1.0), (bc, 1.0), (ac, -1.0)):
            length = jnp.sqrt(dot(edge, edge))
            scale = 1.0 / length
            along = [v * scale for v in edge]
            inside = cross(normal, along) if sign > 0 else cross(along, normal)
            tangents.append(along)
            insides.append(inside)
            lengths.append(0.5 * length)
        functions = [
            list(tangents[0]) + [-dot(a, tangents[0]) - lengths[0]],
            list(insides[0]) + [-dot(a, insides[0])],
            list(normal) + [-dot(a, normal)],
            list(tangents[1]) + [-dot(b, tangents[1]) - lengths[1]],
            list(insides[1]) + [-dot(b, insides[1])],
            list(tangents[2]) + [-dot(a, tangents[2]) - lengths[2]],
            list(insides[2]) + [-dot(a, insides[2])],
        ]
        values = [value for function in functions for value in function] + lengths
        for index, value in enumerate(values):
            table[pl.ds(pl.multiple_of((place * 32 + index) * rows, 8), rows), :] = value
        low = [jnp.min(jnp.minimum(jnp.minimum(a[k], b[k]), c[k]), axis=1, keepdims=True) for k in range(3)]
        high = [jnp.max(jnp.maximum(jnp.maximum(a[k], b[k]), c[k]), axis=1, keepdims=True) for k in range(3)]
        center = [0.5 * (low[k] + high[k]) for k in range(3)]
        squares = []
        for vertex in corners:
            diff = [vertex[k] - center[k] for k in range(3)]
            squares.append(dot(diff, diff))
        far = jnp.max(jnp.maximum(jnp.maximum(squares[0], squares[1]), squares[2]), axis=1, keepdims=True)
        close = jnp.min(jnp.minimum(jnp.minimum(squares[0], squares[1]), squares[2]), axis=1, keepdims=True)
        sphere = jnp.zeros((rows, LANES), jnp.float32)
        for index, value in enumerate(center + [jnp.sqrt(far), jnp.sqrt(close)]):
            sphere = jnp.where(lane_ids == index, value, sphere)
        spheres[pl.ds(pl.multiple_of(place * rows, rows), rows), :] = sphere

    def load_low(dev, carry):
        load_device(dev, low_ref, low_ids, 0)
        return carry

    def load_high(dev, carry):
        load_device(dev, high_ref, high_ids, half_dev)
        return carry

    lax.fori_loop(0, half_dev, load_low, 0, unroll=4)
    lax.fori_loop(0, half_dev, load_high, 0, unroll=4)

    dense_rows = slots * chunks
    dense_lane = lax.broadcasted_iota(jnp.int32, (dense_rows, LANES), 1)
    dense_slot = lax.broadcasted_iota(jnp.int32, (dense_rows, LANES), 0) // chunks

    def find_active(block, found):
        start = pl.multiple_of(block * LANES, LANES)
        here = moved_ref[:, pl.ds(start, LANES)]
        flags = flags_ref[pl.ds(lax.axis_index("surf") * blocks + block, 1), :]
        half = jnp.concatenate([here, jnp.ones((1, LANES), jnp.float32)], axis=0)
        left = stack6(parts3(jnp.concatenate([half, half], axis=0)), LEFT)
        lefts[block] = jnp.transpose(left).astype(jnp.bfloat16)
        nearest[block] = jnp.full((LANES, LANES), big_value, jnp.float32)
        pieces = []
        for slot in range(slots):
            place = jnp.maximum(meta_ref[block, slot], 0)
            pieces.append(spheres[pl.ds(place * chunks, chunks), :])
        tile = jnp.concatenate(pieces, axis=0)
        cx, cy, cz, radius, close = (tile[:, k : k + 1] for k in range(5))
        dx, dy, dz = cx - here[0:1], cy - here[1:2], cz - here[2:3]
        distance = jnp.sqrt(dx * dx + dy * dy + dz * dz)
        real = dense_slot < meta_ref[block, slots]
        upper = jnp.min(jnp.where(real, distance + close, big_value), axis=0, keepdims=True)
        limit = jnp.where(flags == 1, upper * 1.0001 + 1e-4, -big_value)
        keep = jnp.where(real & (distance - radius <= limit), 1.0, 0.0)
        return jnp.where(dense_lane == block, jnp.max(keep, axis=1, keepdims=True), found)

    found = jnp.zeros((dense_rows, LANES), jnp.float32)
    active[...] = lax.fori_loop(0, blocks, find_active, found, unroll=4).astype(jnp.int32)
    copy = pltpu.make_async_copy(active, active_scalars, sem)
    copy.start()
    copy.wait()

    shift = (blocks - 1).bit_length()
    scale = 1 << shift

    def list_block(block, items):
        def list_leaves(group, items):
            for k in range(LIST_SLOTS):
                slot = group * LIST_SLOTS + k
                place = jnp.maximum(meta_ref[block, jnp.minimum(slot, slots - 1)], 0)
                row = divide(place, leaf_dev) * (32 * rows - leaf_dev * chunks) + place * chunks
                code = (row << shift) + block
                for chunk in range(chunks):
                    work[items] = code + (chunk << shift)
                    items = items + active_scalars[slot * chunks + chunk, block]
            return items

        count = jnp.where(meta_ref[block, slots + 1] > 0, meta_ref[block, slots], 0)
        return lax.fori_loop(0, divide(count + LIST_SLOTS - 1, LIST_SLOTS), list_leaves, items)

    items = lax.fori_loop(0, blocks, list_block, 0)
    upper_rows = lax.broadcasted_iota(jnp.int32, (8, LANES), 0) < 4

    def split(code):
        return code & (scale - 1), lax.shift_right_logical(code, shift)

    def right_side(code):
        first = split(code)[1]
        tiles = []
        for pair in range((FUNCS + 1) // 2):
            parts = parts3(table[pl.ds(first + pair * 8 * rows, 8, stride=rows), :])
            for index in range(2):
                if pair * 2 + index < FUNCS:
                    mine = upper_rows if index == 0 else jnp.logical_not(upper_rows)
                    own = [jnp.where(mine, part, 0.0) for part in parts]
                    tiles.append(stack6(own, RIGHT))
        return jnp.concatenate(tiles, axis=1).astype(jnp.bfloat16)

    def products(block, right):
        return jnp.dot(lefts[block], right, preferred_element_type=jnp.float32)

    def evaluate(item, source):
        block, start = split(work[item])
        half_a, half_b, half_c = (
            jnp.broadcast_to(table[pl.ds(start + (28 + k) * rows, 1), :], (8, LANES)) for k in range(3)
        )
        for part in range(LANES // 8):
            here = slice(part * 8, part * 8 + 8)
            ta, sa, h, tb, sb, tc, sc = (
                source[here, k * LANES : (k + 1) * LANES] for k in range(FUNCS)
            )
            over_a = jnp.maximum(jnp.abs(ta) - half_a, 0.0)
            over_b = jnp.maximum(jnp.abs(tb) - half_b, 0.0)
            over_c = jnp.maximum(jnp.abs(tc) - half_c, 0.0)
            edge = jnp.minimum(sa * sa + over_a * over_a, sb * sb + over_b * over_b)
            edge = jnp.minimum(edge, sc * sc + over_c * over_c)
            inside = jnp.minimum(jnp.minimum(sa, sb), sc) >= 0.0
            square = jnp.where(inside, 0.0, edge) + h * h
            nearest[block, here] = jnp.minimum(nearest[block, here], square)

    @pl.when(items > 0)
    def _():
        for extra in range(3 * TOGETHER):
            work[items + extra] = work[items - 1]
        def product(code, right):
            return products(split(code)[0], right)

        for k in range(TOGETHER):
            products_of[k] = product(work[k], right_side(work[k]))
            rights[k] = right_side(work[TOGETHER + k])

        def some_items(step, carry):
            item = step * TOGETHER
            for k in range(TOGETHER):
                coming = product(work[item + TOGETHER + k], rights[k])
                evaluate(item + k, products_of.at[k])
                products_of[k] = coming
                rights[k] = right_side(work[item + 2 * TOGETHER + k])
            return carry

        lax.fori_loop(0, lax.div(items + TOGETHER - 1, TOGETHER), some_items, 0)

    def finish(block, carry):
        square = jnp.min(jnp.transpose(nearest[block]), axis=0, keepdims=True)
        flags = flags_ref[pl.ds(lax.axis_index("surf") * blocks + block, 1), :]
        wall_ref[pl.ds(block, 1), :] = jnp.where(flags == 1, jnp.sqrt(square), 0.0)
        return carry

    lax.fori_loop(0, blocks, finish, 0, unroll=2)


def vmem_params(scratch, operands):
    total = 0
    for ref in scratch:
        if getattr(ref, "memory_space", None) == pltpu.VMEM:
            rows, lanes = ref.shape[-2], ref.shape[-1]
            size = -(-rows // 16) * 16 * -(-lanes // LANES) * LANES * jnp.dtype(ref.dtype).itemsize
            for extent in ref.shape[:-2]:
                size *= extent
            total += size
    for operand in operands:
        total += 2 * operand.size * operand.dtype.itemsize
    return pltpu.CompilerParams(vmem_limit_bytes=min(total + 8 * 1024 * 1024, 60 * 1024 * 1024))


def gather_order(vol_count, surf_count):
    steps = []
    bit = surf_count // 2
    while bit >= 1:
        steps.append(("surf", bit))
        bit //= 2
    bit = vol_count // 2
    while bit >= 1:
        steps.append(("vol", bit))
        bit //= 2
    return steps


def body(surface_points, surface_shift, facet_nodes, volume_points, near_wall, candidates):
    surf_count, vol_count = lax.axis_size("surf"), lax.axis_size("vol")
    sizes = {"surf": surf_count, "vol": vol_count}
    leaf_dev, _, facet_len = facet_nodes.shape
    leaf_len = surface_points.shape[1] // leaf_dev
    halves, chunks = leaf_len // LANES, facet_len // LANES
    devices = surf_count * vol_count
    leaves = devices * leaf_dev
    slots = candidates.shape[1]
    blocks = candidates.shape[0] // surf_count
    share_len = volume_points.shape[1] // surf_count
    rows = leaf_dev * chunks
    payload_rows = leaf_dev * halves * 8 + 3 * rows
    vmem = pl.BlockSpec(memory_space=pltpu.VMEM)
    smem = pl.BlockSpec(memory_space=pltpu.SMEM)

    flag_rows = near_wall.reshape(-1, LANES)
    steps = gather_order(vol_count, surf_count)
    held, meta = pl.pallas_call(
        functools.partial(prep_kernel, steps, surf_count),
        out_shape=[
            jax.ShapeDtypeStruct((1, payload_rows, LANES), jnp.float32),
            jax.ShapeDtypeStruct((blocks, slots + 2), jnp.int32),
        ],
        in_specs=[vmem] * 5,
        out_specs=[vmem] * 2,
        scratch_shapes=[pltpu.VMEM(candidates.shape, jnp.int32)],
    )(surface_points, surface_shift, jnp.transpose(facet_nodes, (1, 0, 2)), flag_rows, jnp.transpose(candidates))
    for axis, bit in steps[:-1]:
        pairs = [(source, source ^ bit) for source in range(sizes[axis])]
        held = jnp.concatenate([held, lax.ppermute(held, axis, pairs)], axis=0)
    axis, bit = steps[-1]
    pairs = [(source, source ^ bit) for source in range(sizes[axis])]
    node_rows = leaf_dev * halves * 8
    held, held_ids = held[:, :node_rows], held[:, node_rows:]
    arrived = lax.ppermute(held, axis, pairs)
    arrived_ids = lax.ppermute(held_ids, axis, pairs)

    groups = -(-leaves // LANES)
    near_scratch = [
        pltpu.VMEM((leaves + 1, 8, leaf_len), jnp.float32),
        pltpu.VMEM((leaves + 1, 48, leaf_len), jnp.bfloat16),
        pltpu.VMEM((leaves + 1, 8, LANES), jnp.float32),
        pltpu.VMEM((8, groups * LANES), jnp.float32),
        pltpu.VMEM((blocks, 4, LANES, LANES), jnp.float32),
        pltpu.VMEM((NEAR_STEPS, NEAR_TOGETHER, LANES, leaf_len), jnp.float32),
        pltpu.VMEM((NEAR_STEPS, NEAR_TOGETHER, LANES, 48), jnp.bfloat16),
        pltpu.SMEM((blocks * (slots // NEAR_TOGETHER + 1) + 3 * NEAR_STEPS,), jnp.int32),
]
    disp, moved = pl.pallas_call(
        functools.partial(near_kernel, leaf_dev, halves),
        out_shape=[jax.ShapeDtypeStruct((3, share_len), jnp.float32)] * 2,
        in_specs=[smem, vmem, vmem, vmem],
        out_specs=[vmem, vmem],
        scratch_shapes=near_scratch,
        compiler_params=vmem_params(near_scratch, (held, arrived, volume_points)),
        cost_estimate=pl.CostEstimate(flops=10**10, bytes_accessed=10**6, transcendentals=10**6),
    )(meta, held, arrived, volume_points)
    wall_scratch = [
        pltpu.VMEM((devices * rows * 32, LANES), jnp.float32),
        pltpu.VMEM((devices * rows, LANES), jnp.float32),
        pltpu.VMEM((blocks, LANES, 48), jnp.bfloat16),
        pltpu.VMEM((blocks, LANES, LANES), jnp.float32),
        pltpu.VMEM((TOGETHER, 48, FUNCS * LANES), jnp.bfloat16),
        pltpu.VMEM((TOGETHER, LANES, FUNCS * LANES), jnp.float32),
        pltpu.VMEM((slots * chunks, LANES), jnp.int32),
        pltpu.SMEM((slots * chunks, LANES), jnp.int32),
        pltpu.SMEM((blocks * slots * chunks + 3 * TOGETHER,), jnp.int32),
        pltpu.SemaphoreType.DMA,
]
    wall = pl.pallas_call(
        functools.partial(wall_kernel, leaf_dev, halves, chunks),
        out_shape=jax.ShapeDtypeStruct((blocks, LANES), jnp.float32),
        in_specs=[smem] + [vmem] * 6,
        out_specs=vmem,
        scratch_shapes=wall_scratch,
        compiler_params=vmem_params(wall_scratch, (held, arrived, held_ids, arrived_ids, flag_rows, volume_points)),
    )(meta, held, arrived, held_ids, arrived_ids, moved, flag_rows)
    return (disp, wall.reshape(-1))


def solution(mesh):
    placed = (
        P(None, ("vol", "surf")),
        P(None, ("vol", "surf")),
        P(("vol", "surf"), None, None),
        P(None, "vol"),
        P("vol"),
        P("vol", None),
    )
    return jax.shard_map(
        body,
        mesh=mesh,
        in_specs=placed,
        out_specs=(P(None, ("vol", "surf")), P(("vol", "surf"))),
        check_vma=False,
    )
```

```python
import functools

import jax
import jax.numpy as jnp
from jax import lax
from jax.experimental import pallas as pl
from jax.experimental.pallas import tpu as pltpu
from jax.sharding import PartitionSpec as P

smoothing = 0.01
big_value = 1e30
LANES = 128
COEFS = 24


def divide(value, by):
    if by & (by - 1) == 0:
        return lax.shift_right_logical(value, jnp.full_like(value, by.bit_length() - 1))
    return lax.div(value, jnp.full_like(value, by))


def prep_kernel(steps, surf_count, points_ref, shift_ref, facets_ref, near_ref, candidates_ref, out_ref, meta_ref, turned):
    corners, leaf_dev, facet_len = facets_ref.shape
    leaf_len = points_ref.shape[1] // leaf_dev
    halves, chunks = leaf_len // LANES, facet_len // LANES
    tail = jnp.where(lax.broadcasted_iota(jnp.int32, (2, LANES), 0) == 0, 1.0, 0.0)
    for leaf in range(leaf_dev):
        for half in range(halves):
            row = (leaf * halves + half) * 8
            lanes = pl.ds((leaf * halves + half) * LANES, LANES)
            out_ref[0, row : row + 3, :] = points_ref[:, lanes]
            out_ref[0, row + 3 : row + 6, :] = shift_ref[:, lanes]
            out_ref[0, row + 6 : row + 8, :] = tail
    base = leaf_dev * halves * 8
    for corner in range(corners):
        ids = facets_ref[corner].astype(jnp.float32)
        for leaf in range(leaf_dev):
            for chunk in range(chunks):
                row = base + (corner * leaf_dev + leaf) * chunks + chunk
                out_ref[0, row : row + 1, :] = ids[leaf : leaf + 1, chunk * LANES : (chunk + 1) * LANES]
    blocks, slots = meta_ref.shape[0], candidates_ref.shape[0]
    turned[...] = jnp.transpose(candidates_ref[...])
    ranks = {"surf": lax.axis_index("surf"), "vol": lax.axis_index("vol")}
    rows = pl.ds(ranks["surf"] * blocks, blocks)
    own = turned[rows, :]
    real = own >= 0
    safe = jnp.maximum(own, 0)
    owner = divide(safe, leaf_dev)
    vol = divide(owner, surf_count)
    apart = {"surf": (owner - vol * surf_count) ^ ranks["surf"], "vol": vol ^ ranks["vol"]}
    place = jnp.zeros_like(own)
    for index, (axis, bit) in enumerate(steps):
        place = place + jnp.where((apart[axis] & bit) != 0, 1 << index, 0)
    place = place * leaf_dev + (safe - owner * leaf_dev)
    meta_ref[:, 0:slots] = jnp.where(real, place, -1)
    count = jnp.sum(jnp.where(real, 1.0, 0.0), axis=1, keepdims=True)
    meta_ref[:, slots : slots + 1] = count.astype(jnp.int32)
    near = jnp.max(near_ref[rows, :].astype(jnp.float32), axis=1, keepdims=True)
    meta_ref[:, slots + 1 : slots + 2] = near.astype(jnp.int32)


def split3(value):
    first = value.astype(jnp.bfloat16)
    rest = value - first.astype(jnp.float32)
    second = rest.astype(jnp.bfloat16)
    third = (rest - second.astype(jnp.float32)).astype(jnp.bfloat16)
    return first, second, third


def stack6(tiles, order):
    return jnp.concatenate([tiles[k] for k in order], axis=0)


def parts3(tile):
    return [part.astype(jnp.float32) for part in split3(tile)]


NEAR_TOGETHER = 2
NEAR_STEPS = 3
LEFT = (0, 0, 0, 1, 1, 2)
RIGHT = (0, 1, 2, 0, 1, 0)


def near_kernel(
    leaf_dev, halves, meta_ref, low_ref, high_ref, volume_ref, disp_ref, moved_ref,
    nodes, rights, middles, moments, acc, ready, lefts, near_work,
):
    half_dev = low_ref.shape[0]
    leaves = nodes.shape[0] - 1
    blocks = disp_ref.shape[1] // LANES
    leaf_len = halves * LANES
    slots = meta_ref.shape[1] - 2
    lane_ids = lax.broadcasted_iota(jnp.int32, (8, LANES), 1)
    row_ids = lax.broadcasted_iota(jnp.int32, (8, LANES), 0)
    groups = moments.shape[1] // LANES

    def right_side(tile, center):
        rows = lax.broadcasted_iota(jnp.int32, tile.shape, 0)
        apart = jnp.where(rows < 3, tile - center, 0.0)
        norm = jnp.sum(apart * apart, axis=0, keepdims=True) + smoothing
        right = jnp.where(rows == 3, 1.0, jnp.where(rows == 4, norm, -2.0 * apart))
        return stack6(parts3(right), RIGHT).astype(jnp.bfloat16)

    def left_side(tile, center):
        offset = jnp.where(row_ids < 3, tile - center, 0.0)
        norm = jnp.sum(offset * offset, axis=0, keepdims=True)
        left = jnp.where(row_ids == 3, norm, jnp.where(row_ids == 4, 1.0, offset))
        return jnp.transpose(stack6(parts3(left), LEFT)).astype(jnp.bfloat16)

    def squares(left, right):
        return jnp.dot(left, right, preferred_element_type=jnp.float32)

    def point_tile(block):
        start = pl.multiple_of((lax.axis_index("surf") * blocks + block) * LANES, LANES)
        here = volume_ref[:, pl.ds(start, LANES)]
        return jnp.concatenate([here, jnp.zeros((5, LANES), jnp.float32)], axis=0)

    moments[...] = jnp.zeros_like(moments)
    nodes[leaves] = jnp.zeros_like(nodes[leaves])
    middles[leaves] = jnp.zeros_like(middles[leaves])
    away = lax.broadcasted_iota(jnp.int32, (48, leaf_len), 0) == 4
    rights[leaves] = jnp.where(away, 1e25, 0.0).astype(jnp.bfloat16)

    def load_device(dev, src_ref, offset):
        for leaf in range(leaf_dev):
            place = (dev + offset) * leaf_dev + leaf
            tiles = []
            for half in range(halves):
                row = (leaf * halves + half) * 8
                tiles.append(src_ref[dev, row : row + 8, :])
            whole = jnp.concatenate(tiles, axis=1)
            nodes[place] = whole
            total = functools.reduce(lambda a, b: a + b, tiles)
            total = jnp.sum(total, axis=1, keepdims=True)
            center = total * (1.0 / leaf_len)
            middles[place] = jnp.broadcast_to(center, (8, LANES))
            rights[place] = right_side(whole, center)
            group = place // LANES
            lanes = pl.ds(pl.multiple_of(group * LANES, LANES), LANES)
            moments[:, lanes] = jnp.where(
                lane_ids == place - group * LANES, total, moments[:, lanes]
            )

    leaf_bits = leaves.bit_length()
    each = -(-blocks // half_dev)

    def list_block(block, items):
        inside = jnp.minimum(block, blocks - 1)
        count = jnp.where(block < blocks, meta_ref[inside, slots], 0)
        for first in range(0, slots, NEAR_TOGETHER):
            code = inside << (NEAR_TOGETHER * leaf_bits)
            for k in range(NEAR_TOGETHER):
                slot = min(first + k, slots - 1)
                place = jnp.where(first + k < count, meta_ref[inside, slot], leaves)
                code = code | (place << (k * leaf_bits))
            near_work[items] = code
            items = items + jnp.where(first < count, 1, 0)
        return items

    def load_low(dev, items):
        load_device(dev, low_ref, 0)
        for k in range(each):
            items = list_block(dev * each + k, items)
        return items

    def load_high(dev, carry):
        load_device(dev, high_ref, half_dev)
        return carry

    items = lax.fori_loop(0, half_dev, load_low, 0, unroll=4)
    lax.fori_loop(0, half_dev, load_high, 0, unroll=4)

    def far_blocks(step, carry):
        here = [step * 2 + k for k in range(2)]
        centers, lefts = [], []
        for block in here:
            tile = point_tile(block)
            center = jnp.sum(tile, axis=1, keepdims=True) * (1.0 / LANES)
            centers.append(center)
            lefts.append(left_side(tile, center))
        for group in range(groups):
            tile = moments[:, group * LANES : (group + 1) * LANES]
            place = lane_ids[:1] + group * LANES
            found = [
                squares(lefts[k], right_side(tile * (1.0 / leaf_len), centers[k])) for k in range(2)
            ]
            for k in range(2):
                listed = place >= leaves
                for slot in range(slots):
                    listed = listed | (place == meta_ref[here[k], slot])
                mask = jnp.where(listed, 0.0, 1.0)
                inverse = 1.0 / found[k]
                weight = inverse * inverse * mask
                for index in range(4):
                    term = weight * tile[3 + index : 4 + index]
                    if group > 0:
                        term = term + acc[here[k], index]
                    acc[here[k], index] = term
        return carry

    lax.fori_loop(0, blocks // 2, far_blocks, 0)

    def step_at(item):
        code = near_work[item]
        mask = (1 << leaf_bits) - 1
        places = tuple(
            lax.shift_right_logical(code, k * leaf_bits) & mask for k in range(NEAR_TOGETHER)
        )
        return lax.shift_right_logical(code, NEAR_TOGETHER * leaf_bits), places

    def pair_lefts(block, places):
        tile = point_tile(block)
        return [left_side(tile, middles[place]) for place in places]

    for extra in range(3 * NEAR_STEPS):
        near_work[items + extra] = sum(leaves << (k * leaf_bits) for k in range(NEAR_TOGETHER))
    states = [step_at(k) for k in range(2 * NEAR_STEPS)]
    for k in range(NEAR_STEPS):
        first = pair_lefts(*states[k])
        coming = pair_lefts(*states[NEAR_STEPS + k])
        for leaf in range(NEAR_TOGETHER):
            ready[k, leaf] = squares(first[leaf], rights[states[k][1][leaf]])
            lefts[k, leaf] = coming[leaf]

    def near_steps(step, carry):
        states = [step_at(step * NEAR_STEPS + k) for k in range(3 * NEAR_STEPS)]
        for k in range(NEAR_STEPS):
            one_step(k, states)
        return carry

    def one_step(k, states):
        block, places = states[k]
        places1 = states[NEAR_STEPS + k][1]
        found = [squares(lefts[k, leaf], rights[places1[leaf]]) for leaf in range(NEAR_TOGETHER)]
        shifts = [
            [
                [
                    jnp.broadcast_to(nodes[place, 3 + axis : 4 + axis, half * LANES : (half + 1) * LANES], (8, LANES))
                    for axis in range(3)
                ]
                for half in range(halves)
            ]
            for place in places
        ]
        for part in range(LANES // 8):
            rows = slice(part * 8, part * 8 + 8)
            total = [None] * 4
            for leaf in range(NEAR_TOGETHER):
                for half in range(halves):
                    inverse = 1.0 / ready[k, leaf, rows, half * LANES : (half + 1) * LANES]
                    weight = inverse * inverse
                    terms = [weight * shifts[leaf][half][axis] for axis in range(3)] + [weight]
                    total = [term if t is None else t + term for t, term in zip(total, terms)]
            for index in range(4):
                acc[block, index, rows] = acc[block, index, rows] + total[index]
        coming = pair_lefts(*states[2 * NEAR_STEPS + k])
        for leaf in range(NEAR_TOGETHER):
            ready[k, leaf] = found[leaf]
            lefts[k, leaf] = coming[leaf]

    lax.fori_loop(0, lax.div(items + NEAR_STEPS - 1, NEAR_STEPS), near_steps, 0)

    def finish(step, carry):
        for k in range(2):
            block = step * 2 + k
            sums = [
                jnp.sum(jnp.transpose(acc[block, index]), axis=0, keepdims=True) for index in range(4)
            ]
            moved_by = jnp.concatenate(sums[:3], axis=0) / sums[3]
            lanes = pl.ds(pl.multiple_of(block * LANES, LANES), LANES)
            start = pl.multiple_of((lax.axis_index("surf") * blocks + block) * LANES, LANES)
            disp_ref[:, lanes] = moved_by
            moved_ref[:, lanes] = volume_ref[:, pl.ds(start, LANES)] + moved_by
        return carry

    lax.fori_loop(0, blocks // 2, finish, 0)


def cross(a, b):
    return (a[1] * b[2] - a[2] * b[1], a[2] * b[0] - a[0] * b[2], a[0] * b[1] - a[1] * b[0])


def dot(a, b):
    return a[0] * b[0] + a[1] * b[1] + a[2] * b[2]


FUNCS = 7
LIST_SLOTS = 4
TOGETHER = 6


def wall_kernel(
    leaf_dev, halves, chunks, meta_ref, low_ref, high_ref, low_ids, high_ids, moved_ref, flags_ref, wall_ref,
    table, spheres, lefts, nearest, rights, products_of,
    active, active_scalars, work, sem,
):
    half_dev = low_ref.shape[0]
    rows = leaf_dev * chunks
    blocks = wall_ref.shape[0]
    slots = meta_ref.shape[1] - 2
    lane_ids = lax.broadcasted_iota(jnp.int32, (rows, LANES), 1)

    def load_device(dev, src_ref, ids_ref, offset):
        place = dev + offset
        moved = []
        for axis in range(3):
            parts = []
            for half in range(halves):
                pieces = []
                for leaf in range(leaf_dev):
                    row = (leaf * halves + half) * 8
                    line = src_ref[dev, row + axis : row + axis + 1, :]
                    line = line + src_ref[dev, row + 3 + axis : row + 4 + axis, :]
                    pieces.append(jnp.broadcast_to(line, (chunks, LANES)))
                parts.append(jnp.concatenate(pieces, axis=0))
            moved.append(parts)
        corners = []
        for corner in range(3):
            ids = ids_ref[dev, corner * rows : (corner + 1) * rows, :].astype(jnp.int32)
            lane = ids & (LANES - 1)
            vertex = []
            for axis in range(3):
                value = jnp.take_along_axis(moved[axis][0], lane, axis=1)
                for half in range(1, halves):
                    other = jnp.take_along_axis(moved[axis][half], lane, axis=1)
                    value = jnp.where(ids >= half * LANES, other, value)
                vertex.append(value)
            corners.append(vertex)
        a, b, c = corners
        ab = [b[k] - a[k] for k in range(3)]
        bc = [c[k] - b[k] for k in range(3)]
        ac = [c[k] - a[k] for k in range(3)]
        normal = cross(ab, ac)
        scale = 1.0 / jnp.sqrt(dot(normal, normal))
        normal = [v * scale for v in normal]
        tangents, insides, lengths = [], [], []
        for edge, sign in ((ab, 1.0), (bc, 1.0), (ac, -1.0)):
            length = jnp.sqrt(dot(edge, edge))
            scale = 1.0 / length
            along = [v * scale for v in edge]
            inside = cross(normal, along) if sign > 0 else cross(along, normal)
            tangents.append(along)
            insides.append(inside)
            lengths.append(0.5 * length)
        functions = [
            list(tangents[0]) + [-dot(a, tangents[0]) - lengths[0]],
            list(insides[0]) + [-dot(a, insides[0])],
            list(normal) + [-dot(a, normal)],
            list(tangents[1]) + [-dot(b, tangents[1]) - lengths[1]],
            list(insides[1]) + [-dot(b, insides[1])],
            list(tangents[2]) + [-dot(a, tangents[2]) - lengths[2]],
            list(insides[2]) + [-dot(a, insides[2])],
        ]
        values = [value for function in functions for value in function] + lengths
        for index, value in enumerate(values):
            table[pl.ds(pl.multiple_of((place * 32 + index) * rows, 8), rows), :] = value
        low = [jnp.min(jnp.minimum(jnp.minimum(a[k], b[k]), c[k]), axis=1, keepdims=True) for k in range(3)]
        high = [jnp.max(jnp.maximum(jnp.maximum(a[k], b[k]), c[k]), axis=1, keepdims=True) for k in range(3)]
        center = [0.5 * (low[k] + high[k]) for k in range(3)]
        squares = []
        for vertex in corners:
            diff = [vertex[k] - center[k] for k in range(3)]
            squares.append(dot(diff, diff))
        far = jnp.max(jnp.maximum(jnp.maximum(squares[0], squares[1]), squares[2]), axis=1, keepdims=True)
        close = jnp.min(jnp.minimum(jnp.minimum(squares[0], squares[1]), squares[2]), axis=1, keepdims=True)
        sphere = jnp.zeros((rows, LANES), jnp.float32)
        for index, value in enumerate(center + [jnp.sqrt(far), jnp.sqrt(close)]):
            sphere = jnp.where(lane_ids == index, value, sphere)
        spheres[pl.ds(pl.multiple_of(place * rows, rows), rows), :] = sphere

    def load_low(dev, carry):
        load_device(dev, low_ref, low_ids, 0)
        return carry

    def load_high(dev, carry):
        load_device(dev, high_ref, high_ids, half_dev)
        return carry

    lax.fori_loop(0, half_dev, load_low, 0, unroll=4)
    lax.fori_loop(0, half_dev, load_high, 0, unroll=4)

    dense_rows = slots * chunks
    dense_lane = lax.broadcasted_iota(jnp.int32, (dense_rows, LANES), 1)
    dense_slot = lax.broadcasted_iota(jnp.int32, (dense_rows, LANES), 0) // chunks

    batch = next(k for k in (4, 2, 1) if blocks % k == 0)

    def find_active(step, found):
        members = [step * batch + k for k in range(batch)]
        tiles, points, limits = [], [], []
        for block in members:
            pieces = []
            for slot in range(slots):
                place = jnp.maximum(meta_ref[block, slot], 0)
                pieces.append(spheres[pl.ds(place * chunks, chunks), :])
            tiles.append(jnp.concatenate(pieces, axis=0))
            start = pl.multiple_of(block * LANES, LANES)
            points.append(moved_ref[:, pl.ds(start, LANES)])
        squares = [None] * batch
        for axis in range(3):
            centers = [jnp.broadcast_to(tile[:, axis : axis + 1], tile.shape) for tile in tiles]
            for k in range(batch):
                diff = centers[k] - points[k][axis : axis + 1]
                squares[k] = diff * diff if axis == 0 else squares[k] + diff * diff
        distances = [jnp.sqrt(square) for square in squares]
        close = [jnp.broadcast_to(tile[:, 4:5], tile.shape) for tile in tiles]
        radius = [jnp.broadcast_to(tile[:, 3:4], tile.shape) for tile in tiles]
        keeps = []
        for k, block in enumerate(members):
            real = dense_slot < meta_ref[block, slots]
            upper = jnp.where(real, distances[k] + close[k], big_value)
            upper = jnp.min(upper, axis=0, keepdims=True)
            flags = flags_ref[pl.ds(lax.axis_index("surf") * blocks + block, 1), :]
            limit = jnp.where(flags == 1, upper * 1.0001 + 1e-4, -big_value)
            keeps.append(jnp.where(real & (distances[k] - radius[k] <= limit), 1.0, 0.0))
        keeps = [jnp.max(keep, axis=1, keepdims=True) for keep in keeps]
        for k, block in enumerate(members):
            found = jnp.where(dense_lane == block, keeps[k], found)
        lefts_here = []
        for k in range(batch):
            half = jnp.concatenate([points[k], jnp.ones((1, LANES), jnp.float32)], axis=0)
            lefts_here.append(stack6(parts3(jnp.concatenate([half, half], axis=0)), LEFT))
        lefts_here = [jnp.transpose(left) for left in lefts_here]
        for k, block in enumerate(members):
            lefts[block] = lefts_here[k].astype(jnp.bfloat16)
            nearest[block] = jnp.full((LANES, LANES), big_value, jnp.float32)
        return found

    found = jnp.zeros((dense_rows, LANES), jnp.float32)
    active[...] = lax.fori_loop(0, blocks // batch, find_active, found).astype(jnp.int32)
    copy = pltpu.make_async_copy(active, active_scalars, sem)
    copy.start()
    copy.wait()

    shift = (blocks - 1).bit_length()
    scale = 1 << shift

    def list_block(block, items):
        def list_leaves(group, items):
            for k in range(LIST_SLOTS):
                slot = group * LIST_SLOTS + k
                place = jnp.maximum(meta_ref[block, jnp.minimum(slot, slots - 1)], 0)
                row = divide(place, leaf_dev) * (32 * rows - leaf_dev * chunks) + place * chunks
                code = (row << shift) + block
                for chunk in range(chunks):
                    work[items] = code + (chunk << shift)
                    items = items + active_scalars[slot * chunks + chunk, block]
            return items

        count = jnp.where(meta_ref[block, slots + 1] > 0, meta_ref[block, slots], 0)
        return lax.fori_loop(0, divide(count + LIST_SLOTS - 1, LIST_SLOTS), list_leaves, items)

    items = lax.fori_loop(0, blocks, list_block, 0)
    upper_rows = lax.broadcasted_iota(jnp.int32, (8, LANES), 0) < 4

    def split(code):
        return code & (scale - 1), lax.shift_right_logical(code, shift)

    def right_side(code):
        first = split(code)[1]
        tiles = []
        for pair in range((FUNCS + 1) // 2):
            parts = parts3(table[pl.ds(first + pair * 8 * rows, 8, stride=rows), :])
            for index in range(2):
                if pair * 2 + index < FUNCS:
                    mine = upper_rows if index == 0 else jnp.logical_not(upper_rows)
                    own = [jnp.where(mine, part, 0.0) for part in parts]
                    tiles.append(stack6(own, RIGHT))
        return jnp.concatenate(tiles, axis=1).astype(jnp.bfloat16)

    def products(block, right):
        return jnp.dot(lefts[block], right, preferred_element_type=jnp.float32)

    def evaluate(item, source):
        block, start = split(work[item])
        half_a, half_b, half_c = (
            jnp.broadcast_to(table[pl.ds(start + (28 + k) * rows, 1), :], (8, LANES)) for k in range(3)
        )
        for part in range(LANES // 8):
            here = slice(part * 8, part * 8 + 8)
            ta, sa, h, tb, sb, tc, sc = (
                source[here, k * LANES : (k + 1) * LANES] for k in range(FUNCS)
            )
            over_a = jnp.maximum(jnp.abs(ta) - half_a, 0.0)
            over_b = jnp.maximum(jnp.abs(tb) - half_b, 0.0)
            over_c = jnp.maximum(jnp.abs(tc) - half_c, 0.0)
            edge = jnp.minimum(sa * sa + over_a * over_a, sb * sb + over_b * over_b)
            edge = jnp.minimum(edge, sc * sc + over_c * over_c)
            inside = jnp.minimum(jnp.minimum(sa, sb), sc) >= 0.0
            square = jnp.where(inside, 0.0, edge) + h * h
            nearest[block, here] = jnp.minimum(nearest[block, here], square)

    @pl.when(items > 0)
    def _():
        for extra in range(3 * TOGETHER):
            work[items + extra] = work[items - 1]
        def product(code, right):
            return products(split(code)[0], right)

        for k in range(TOGETHER):
            products_of[k] = product(work[k], right_side(work[k]))
            rights[k] = right_side(work[TOGETHER + k])

        def some_items(step, carry):
            item = step * TOGETHER
            for k in range(TOGETHER):
                coming = product(work[item + TOGETHER + k], rights[k])
                evaluate(item + k, products_of.at[k])
                products_of[k] = coming
                rights[k] = right_side(work[item + 2 * TOGETHER + k])
            return carry

        lax.fori_loop(0, lax.div(items + TOGETHER - 1, TOGETHER), some_items, 0)

    def finish(block, carry):
        square = jnp.min(jnp.transpose(nearest[block]), axis=0, keepdims=True)
        flags = flags_ref[pl.ds(lax.axis_index("surf") * blocks + block, 1), :]
        wall_ref[pl.ds(block, 1), :] = jnp.where(flags == 1, jnp.sqrt(square), 0.0)
        return carry

    lax.fori_loop(0, blocks, finish, 0, unroll=2)


def vmem_params(scratch, operands):
    total = 0
    for ref in scratch:
        if getattr(ref, "memory_space", None) == pltpu.VMEM:
            rows, lanes = ref.shape[-2], ref.shape[-1]
            size = -(-rows // 16) * 16 * -(-lanes // LANES) * LANES * jnp.dtype(ref.dtype).itemsize
            for extent in ref.shape[:-2]:
                size *= extent
            total += size
    for operand in operands:
        total += 2 * operand.size * operand.dtype.itemsize
    return pltpu.CompilerParams(vmem_limit_bytes=min(total + 8 * 1024 * 1024, 60 * 1024 * 1024))


def gather_order(vol_count, surf_count):
    steps = []
    bit = surf_count // 2
    while bit >= 1:
        steps.append(("surf", bit))
        bit //= 2
    bit = vol_count // 2
    while bit >= 1:
        steps.append(("vol", bit))
        bit //= 2
    return steps


def body(surface_points, surface_shift, facet_nodes, volume_points, near_wall, candidates):
    surf_count, vol_count = lax.axis_size("surf"), lax.axis_size("vol")
    sizes = {"surf": surf_count, "vol": vol_count}
    leaf_dev, _, facet_len = facet_nodes.shape
    leaf_len = surface_points.shape[1] // leaf_dev
    halves, chunks = leaf_len // LANES, facet_len // LANES
    devices = surf_count * vol_count
    leaves = devices * leaf_dev
    slots = candidates.shape[1]
    blocks = candidates.shape[0] // surf_count
    share_len = volume_points.shape[1] // surf_count
    rows = leaf_dev * chunks
    payload_rows = leaf_dev * halves * 8 + 3 * rows
    vmem = pl.BlockSpec(memory_space=pltpu.VMEM)
    smem = pl.BlockSpec(memory_space=pltpu.SMEM)

    flag_rows = near_wall.reshape(-1, LANES)
    steps = gather_order(vol_count, surf_count)
    held, meta = pl.pallas_call(
        functools.partial(prep_kernel, steps, surf_count),
        out_shape=[
            jax.ShapeDtypeStruct((1, payload_rows, LANES), jnp.float32),
            jax.ShapeDtypeStruct((blocks, slots + 2), jnp.int32),
        ],
        in_specs=[vmem] * 5,
        out_specs=[vmem] * 2,
        scratch_shapes=[pltpu.VMEM(candidates.shape, jnp.int32)],
    )(surface_points, surface_shift, jnp.transpose(facet_nodes, (1, 0, 2)), flag_rows, jnp.transpose(candidates))
    for axis, bit in steps[:-1]:
        pairs = [(source, source ^ bit) for source in range(sizes[axis])]
        held = jnp.concatenate([held, lax.ppermute(held, axis, pairs)], axis=0)
    axis, bit = steps[-1]
    pairs = [(source, source ^ bit) for source in range(sizes[axis])]
    node_rows = leaf_dev * halves * 8
    held, held_ids = held[:, :node_rows], held[:, node_rows:]
    arrived = lax.ppermute(held, axis, pairs)
    arrived_ids = lax.ppermute(held_ids, axis, pairs)

    groups = -(-leaves // LANES)
    near_scratch = [
        pltpu.VMEM((leaves + 1, 8, leaf_len), jnp.float32),
        pltpu.VMEM((leaves + 1, 48, leaf_len), jnp.bfloat16),
        pltpu.VMEM((leaves + 1, 8, LANES), jnp.float32),
        pltpu.VMEM((8, groups * LANES), jnp.float32),
        pltpu.VMEM((blocks, 4, LANES, LANES), jnp.float32),
        pltpu.VMEM((NEAR_STEPS, NEAR_TOGETHER, LANES, leaf_len), jnp.float32),
        pltpu.VMEM((NEAR_STEPS, NEAR_TOGETHER, LANES, 48), jnp.bfloat16),
        pltpu.SMEM((blocks * (slots // NEAR_TOGETHER + 1) + 3 * NEAR_STEPS,), jnp.int32),
]
    disp, moved = pl.pallas_call(
        functools.partial(near_kernel, leaf_dev, halves),
        out_shape=[jax.ShapeDtypeStruct((3, share_len), jnp.float32)] * 2,
        in_specs=[smem, vmem, vmem, vmem],
        out_specs=[vmem, vmem],
        scratch_shapes=near_scratch,
        compiler_params=vmem_params(near_scratch, (held, arrived, volume_points)),
        cost_estimate=pl.CostEstimate(flops=10**10, bytes_accessed=10**6, transcendentals=10**6),
    )(meta, held, arrived, volume_points)
    wall_scratch = [
        pltpu.VMEM((devices * rows * 32, LANES), jnp.float32),
        pltpu.VMEM((devices * rows, LANES), jnp.float32),
        pltpu.VMEM((blocks, LANES, 48), jnp.bfloat16),
        pltpu.VMEM((blocks, LANES, LANES), jnp.float32),
        pltpu.VMEM((TOGETHER, 48, FUNCS * LANES), jnp.bfloat16),
        pltpu.VMEM((TOGETHER, LANES, FUNCS * LANES), jnp.float32),
        pltpu.VMEM((slots * chunks, LANES), jnp.int32),
        pltpu.SMEM((slots * chunks, LANES), jnp.int32),
        pltpu.SMEM((blocks * slots * chunks + 3 * TOGETHER,), jnp.int32),
        pltpu.SemaphoreType.DMA,
]
    wall = pl.pallas_call(
        functools.partial(wall_kernel, leaf_dev, halves, chunks),
        out_shape=jax.ShapeDtypeStruct((blocks, LANES), jnp.float32),
        in_specs=[smem] + [vmem] * 6,
        out_specs=vmem,
        scratch_shapes=wall_scratch,
        compiler_params=vmem_params(wall_scratch, (held, arrived, held_ids, arrived_ids, flag_rows, volume_points)),
    )(meta, held, arrived, held_ids, arrived_ids, moved, flag_rows)
    return (disp, wall.reshape(-1))


def solution(mesh):
    placed = (
        P(None, ("vol", "surf")),
        P(None, ("vol", "surf")),
        P(("vol", "surf"), None, None),
        P(None, "vol"),
        P("vol"),
        P("vol", None),
    )
    return jax.shard_map(
        body,
        mesh=mesh,
        in_specs=placed,
        out_specs=(P(None, ("vol", "surf")), P(("vol", "surf"))),
        check_vma=False,
    )
```

```python
import functools

import jax
import jax.numpy as jnp
from jax import lax
from jax.experimental import pallas as pl
from jax.experimental.pallas import tpu as pltpu
from jax.sharding import PartitionSpec as P

smoothing = 0.01
big_value = 1e30
LANES = 128
COEFS = 24


def divide(value, by):
    if by & (by - 1) == 0:
        return lax.shift_right_logical(value, jnp.full_like(value, by.bit_length() - 1))
    return lax.div(value, jnp.full_like(value, by))


def prep_kernel(steps, surf_count, points_ref, shift_ref, facets_ref, near_ref, candidates_ref, out_ref, meta_ref, turned):
    corners, leaf_dev, facet_len = facets_ref.shape
    leaf_len = points_ref.shape[1] // leaf_dev
    halves, chunks = leaf_len // LANES, facet_len // LANES
    tail = jnp.where(lax.broadcasted_iota(jnp.int32, (2, LANES), 0) == 0, 1.0, 0.0)
    for leaf in range(leaf_dev):
        for half in range(halves):
            row = (leaf * halves + half) * 8
            lanes = pl.ds((leaf * halves + half) * LANES, LANES)
            out_ref[0, row : row + 3, :] = points_ref[:, lanes]
            out_ref[0, row + 3 : row + 6, :] = shift_ref[:, lanes]
            out_ref[0, row + 6 : row + 8, :] = tail
    base = leaf_dev * halves * 8
    for corner in range(corners):
        ids = facets_ref[corner].astype(jnp.float32)
        for leaf in range(leaf_dev):
            for chunk in range(chunks):
                row = base + (corner * leaf_dev + leaf) * chunks + chunk
                out_ref[0, row : row + 1, :] = ids[leaf : leaf + 1, chunk * LANES : (chunk + 1) * LANES]
    blocks, slots = meta_ref.shape[0], candidates_ref.shape[0]
    turned[...] = jnp.transpose(candidates_ref[...])
    ranks = {"surf": lax.axis_index("surf"), "vol": lax.axis_index("vol")}
    rows = pl.ds(ranks["surf"] * blocks, blocks)
    own = turned[rows, :]
    real = own >= 0
    safe = jnp.maximum(own, 0)
    owner = divide(safe, leaf_dev)
    vol = divide(owner, surf_count)
    apart = {"surf": (owner - vol * surf_count) ^ ranks["surf"], "vol": vol ^ ranks["vol"]}
    place = jnp.zeros_like(own)
    for index, (axis, bit) in enumerate(steps):
        place = place + jnp.where((apart[axis] & bit) != 0, 1 << index, 0)
    place = place * leaf_dev + (safe - owner * leaf_dev)
    meta_ref[:, 0:slots] = jnp.where(real, place, -1)
    count = jnp.sum(jnp.where(real, 1.0, 0.0), axis=1, keepdims=True)
    meta_ref[:, slots : slots + 1] = count.astype(jnp.int32)
    near = jnp.max(near_ref[rows, :].astype(jnp.float32), axis=1, keepdims=True)
    meta_ref[:, slots + 1 : slots + 2] = near.astype(jnp.int32)


def split3(value):
    first = value.astype(jnp.bfloat16)
    rest = value - first.astype(jnp.float32)
    second = rest.astype(jnp.bfloat16)
    third = (rest - second.astype(jnp.float32)).astype(jnp.bfloat16)
    return first, second, third


def stack6(tiles, order):
    return jnp.concatenate([tiles[k] for k in order], axis=0)


def parts3(tile):
    return [part.astype(jnp.float32) for part in split3(tile)]


NEAR_TOGETHER = 2
NEAR_STEPS = 4
LEFT = (0, 0, 0, 1, 1, 2)
RIGHT = (0, 1, 2, 0, 1, 0)


def near_kernel(
    leaf_dev, halves, meta_ref, low_ref, high_ref, volume_ref, disp_ref, moved_ref,
    nodes, rights, middles, moments, acc, ready, lefts, near_work,
):
    half_dev = low_ref.shape[0]
    leaves = nodes.shape[0] - 1
    blocks = disp_ref.shape[1] // LANES
    leaf_len = halves * LANES
    slots = meta_ref.shape[1] - 2
    lane_ids = lax.broadcasted_iota(jnp.int32, (8, LANES), 1)
    row_ids = lax.broadcasted_iota(jnp.int32, (8, LANES), 0)
    groups = moments.shape[1] // LANES

    def right_side(tile, center):
        rows = lax.broadcasted_iota(jnp.int32, tile.shape, 0)
        apart = jnp.where(rows < 3, tile - center, 0.0)
        norm = jnp.sum(apart * apart, axis=0, keepdims=True) + smoothing
        right = jnp.where(rows == 3, 1.0, jnp.where(rows == 4, norm, -2.0 * apart))
        return stack6(parts3(right), RIGHT).astype(jnp.bfloat16)

    def left_side(tile, center):
        offset = jnp.where(row_ids < 3, tile - center, 0.0)
        norm = jnp.sum(offset * offset, axis=0, keepdims=True)
        left = jnp.where(row_ids == 3, norm, jnp.where(row_ids == 4, 1.0, offset))
        return jnp.transpose(stack6(parts3(left), LEFT)).astype(jnp.bfloat16)

    def squares(left, right):
        return jnp.dot(left, right, preferred_element_type=jnp.float32)

    def point_tile(block):
        start = pl.multiple_of((lax.axis_index("surf") * blocks + block) * LANES, LANES)
        here = volume_ref[:, pl.ds(start, LANES)]
        return jnp.concatenate([here, jnp.zeros((5, LANES), jnp.float32)], axis=0)

    moments[...] = jnp.zeros_like(moments)
    nodes[leaves] = jnp.zeros_like(nodes[leaves])
    middles[leaves] = jnp.zeros_like(middles[leaves])
    away = lax.broadcasted_iota(jnp.int32, (48, leaf_len), 0) == 4
    rights[leaves] = jnp.where(away, 1e25, 0.0).astype(jnp.bfloat16)

    def load_device(dev, src_ref, offset):
        for leaf in range(leaf_dev):
            place = (dev + offset) * leaf_dev + leaf
            tiles = []
            for half in range(halves):
                row = (leaf * halves + half) * 8
                tiles.append(src_ref[dev, row : row + 8, :])
            whole = jnp.concatenate(tiles, axis=1)
            nodes[place] = whole
            total = functools.reduce(lambda a, b: a + b, tiles)
            total = jnp.sum(total, axis=1, keepdims=True)
            center = total * (1.0 / leaf_len)
            middles[place] = jnp.broadcast_to(center, (8, LANES))
            rights[place] = right_side(whole, center)
            group = place // LANES
            lanes = pl.ds(pl.multiple_of(group * LANES, LANES), LANES)
            moments[:, lanes] = jnp.where(
                lane_ids == place - group * LANES, total, moments[:, lanes]
            )

    leaf_bits = leaves.bit_length()
    each = -(-blocks // half_dev)

    def list_block(block, items):
        inside = jnp.minimum(block, blocks - 1)
        count = jnp.where(block < blocks, meta_ref[inside, slots], 0)
        for first in range(0, slots, NEAR_TOGETHER):
            code = inside << (NEAR_TOGETHER * leaf_bits)
            for k in range(NEAR_TOGETHER):
                slot = min(first + k, slots - 1)
                place = jnp.where(first + k < count, meta_ref[inside, slot], leaves)
                code = code | (place << (k * leaf_bits))
            near_work[items] = code
            items = items + jnp.where(first < count, 1, 0)
        return items

    def load_low(dev, items):
        load_device(dev, low_ref, 0)
        for k in range(each):
            items = list_block(dev * each + k, items)
        return items

    def load_high(dev, carry):
        load_device(dev, high_ref, half_dev)
        return carry

    items = lax.fori_loop(0, half_dev, load_low, 0, unroll=4)
    lax.fori_loop(0, half_dev, load_high, 0, unroll=4)

    def far_blocks(step, carry):
        here = [step * 2 + k for k in range(2)]
        centers, lefts = [], []
        for block in here:
            tile = point_tile(block)
            center = jnp.sum(tile, axis=1, keepdims=True) * (1.0 / LANES)
            centers.append(center)
            lefts.append(left_side(tile, center))
        for group in range(groups):
            tile = moments[:, group * LANES : (group + 1) * LANES]
            place = lane_ids[:1] + group * LANES
            found = [
                squares(lefts[k], right_side(tile * (1.0 / leaf_len), centers[k])) for k in range(2)
            ]
            for k in range(2):
                listed = place >= leaves
                for slot in range(slots):
                    listed = listed | (place == meta_ref[here[k], slot])
                mask = jnp.where(listed, 0.0, 1.0)
                inverse = 1.0 / found[k]
                weight = inverse * inverse * mask
                for index in range(4):
                    term = weight * tile[3 + index : 4 + index]
                    if group > 0:
                        term = term + acc[here[k], index]
                    acc[here[k], index] = term
        return carry

    lax.fori_loop(0, blocks // 2, far_blocks, 0)

    def step_at(item):
        code = near_work[item]
        mask = (1 << leaf_bits) - 1
        places = tuple(
            lax.shift_right_logical(code, k * leaf_bits) & mask for k in range(NEAR_TOGETHER)
        )
        return lax.shift_right_logical(code, NEAR_TOGETHER * leaf_bits), places

    def pair_lefts(block, places):
        tile = point_tile(block)
        return [left_side(tile, middles[place]) for place in places]

    for extra in range(3 * NEAR_STEPS):
        near_work[items + extra] = sum(leaves << (k * leaf_bits) for k in range(NEAR_TOGETHER))
    states = [step_at(k) for k in range(2 * NEAR_STEPS)]
    for k in range(NEAR_STEPS):
        first = pair_lefts(*states[k])
        coming = pair_lefts(*states[NEAR_STEPS + k])
        for leaf in range(NEAR_TOGETHER):
            ready[k, leaf] = squares(first[leaf], rights[states[k][1][leaf]])
            lefts[k, leaf] = coming[leaf]

    def near_steps(step, carry):
        states = [step_at(step * NEAR_STEPS + k) for k in range(3 * NEAR_STEPS)]
        for k in range(NEAR_STEPS):
            one_step(k, states)
        return carry

    def one_step(k, states):
        block, places = states[k]
        places1 = states[NEAR_STEPS + k][1]
        found = [squares(lefts[k, leaf], rights[places1[leaf]]) for leaf in range(NEAR_TOGETHER)]
        shifts = [
            [
                [
                    jnp.broadcast_to(nodes[place, 3 + axis : 4 + axis, half * LANES : (half + 1) * LANES], (8, LANES))
                    for axis in range(3)
                ]
                for half in range(halves)
            ]
            for place in places
        ]
        for part in range(LANES // 8):
            rows = slice(part * 8, part * 8 + 8)
            total = [None] * 4
            for leaf in range(NEAR_TOGETHER):
                for half in range(halves):
                    inverse = 1.0 / ready[k, leaf, rows, half * LANES : (half + 1) * LANES]
                    weight = inverse * inverse
                    terms = [weight * shifts[leaf][half][axis] for axis in range(3)] + [weight]
                    total = [term if t is None else t + term for t, term in zip(total, terms)]
            for index in range(4):
                acc[block, index, rows] = acc[block, index, rows] + total[index]
        coming = pair_lefts(*states[2 * NEAR_STEPS + k])
        for leaf in range(NEAR_TOGETHER):
            ready[k, leaf] = found[leaf]
            lefts[k, leaf] = coming[leaf]

    lax.fori_loop(0, lax.div(items + NEAR_STEPS - 1, NEAR_STEPS), near_steps, 0)

    def finish(step, carry):
        for k in range(2):
            block = step * 2 + k
            sums = [
                jnp.sum(jnp.transpose(acc[block, index]), axis=0, keepdims=True) for index in range(4)
            ]
            moved_by = jnp.concatenate(sums[:3], axis=0) / sums[3]
            lanes = pl.ds(pl.multiple_of(block * LANES, LANES), LANES)
            start = pl.multiple_of((lax.axis_index("surf") * blocks + block) * LANES, LANES)
            disp_ref[:, lanes] = moved_by
            moved_ref[:, lanes] = volume_ref[:, pl.ds(start, LANES)] + moved_by
        return carry

    lax.fori_loop(0, blocks // 2, finish, 0)


def cross(a, b):
    return (a[1] * b[2] - a[2] * b[1], a[2] * b[0] - a[0] * b[2], a[0] * b[1] - a[1] * b[0])


def dot(a, b):
    return a[0] * b[0] + a[1] * b[1] + a[2] * b[2]


FUNCS = 7
LIST_SLOTS = 4
TOGETHER = 6


def wall_kernel(
    leaf_dev, halves, chunks, meta_ref, low_ref, high_ref, low_ids, high_ids, moved_ref, flags_ref, wall_ref,
    table, spheres, lefts, nearest, rights, products_of,
    active, active_scalars, work, sem,
):
    half_dev = low_ref.shape[0]
    rows = leaf_dev * chunks
    blocks = wall_ref.shape[0]
    slots = meta_ref.shape[1] - 2
    lane_ids = lax.broadcasted_iota(jnp.int32, (rows, LANES), 1)

    def load_device(dev, src_ref, ids_ref, offset):
        place = dev + offset
        moved = []
        for axis in range(3):
            parts = []
            for half in range(halves):
                pieces = []
                for leaf in range(leaf_dev):
                    row = (leaf * halves + half) * 8
                    line = src_ref[dev, row + axis : row + axis + 1, :]
                    line = line + src_ref[dev, row + 3 + axis : row + 4 + axis, :]
                    pieces.append(jnp.broadcast_to(line, (chunks, LANES)))
                parts.append(jnp.concatenate(pieces, axis=0))
            moved.append(parts)
        corners = []
        for corner in range(3):
            ids = ids_ref[dev, corner * rows : (corner + 1) * rows, :].astype(jnp.int32)
            lane = ids & (LANES - 1)
            vertex = []
            for axis in range(3):
                value = jnp.take_along_axis(moved[axis][0], lane, axis=1)
                for half in range(1, halves):
                    other = jnp.take_along_axis(moved[axis][half], lane, axis=1)
                    value = jnp.where(ids >= half * LANES, other, value)
                vertex.append(value)
            corners.append(vertex)
        a, b, c = corners
        ab = [b[k] - a[k] for k in range(3)]
        bc = [c[k] - b[k] for k in range(3)]
        ac = [c[k] - a[k] for k in range(3)]
        normal = cross(ab, ac)
        scale = 1.0 / jnp.sqrt(dot(normal, normal))
        normal = [v * scale for v in normal]
        tangents, insides, lengths = [], [], []
        for edge, sign in ((ab, 1.0), (bc, 1.0), (ac, -1.0)):
            length = jnp.sqrt(dot(edge, edge))
            scale = 1.0 / length
            along = [v * scale for v in edge]
            inside = cross(normal, along) if sign > 0 else cross(along, normal)
            tangents.append(along)
            insides.append(inside)
            lengths.append(0.5 * length)
        functions = [
            list(tangents[0]) + [-dot(a, tangents[0]) - lengths[0]],
            list(insides[0]) + [-dot(a, insides[0])],
            list(normal) + [-dot(a, normal)],
            list(tangents[1]) + [-dot(b, tangents[1]) - lengths[1]],
            list(insides[1]) + [-dot(b, insides[1])],
            list(tangents[2]) + [-dot(a, tangents[2]) - lengths[2]],
            list(insides[2]) + [-dot(a, insides[2])],
        ]
        values = [value for function in functions for value in function] + lengths
        for index, value in enumerate(values):
            table[pl.ds(pl.multiple_of((place * 32 + index) * rows, 8), rows), :] = value
        low = [jnp.min(jnp.minimum(jnp.minimum(a[k], b[k]), c[k]), axis=1, keepdims=True) for k in range(3)]
        high = [jnp.max(jnp.maximum(jnp.maximum(a[k], b[k]), c[k]), axis=1, keepdims=True) for k in range(3)]
        center = [0.5 * (low[k] + high[k]) for k in range(3)]
        squares = []
        for vertex in corners:
            diff = [vertex[k] - center[k] for k in range(3)]
            squares.append(dot(diff, diff))
        far = jnp.max(jnp.maximum(jnp.maximum(squares[0], squares[1]), squares[2]), axis=1, keepdims=True)
        close = jnp.min(jnp.minimum(jnp.minimum(squares[0], squares[1]), squares[2]), axis=1, keepdims=True)
        sphere = jnp.zeros((rows, LANES), jnp.float32)
        for index, value in enumerate(center + [jnp.sqrt(far), jnp.sqrt(close)]):
            sphere = jnp.where(lane_ids == index, value, sphere)
        spheres[pl.ds(pl.multiple_of(place * rows, rows), rows), :] = sphere

    def load_low(dev, carry):
        load_device(dev, low_ref, low_ids, 0)
        return carry

    def load_high(dev, carry):
        load_device(dev, high_ref, high_ids, half_dev)
        return carry

    lax.fori_loop(0, half_dev, load_low, 0, unroll=4)
    lax.fori_loop(0, half_dev, load_high, 0, unroll=4)

    dense_rows = slots * chunks
    dense_lane = lax.broadcasted_iota(jnp.int32, (dense_rows, LANES), 1)
    dense_slot = lax.broadcasted_iota(jnp.int32, (dense_rows, LANES), 0) // chunks

    batch = next(k for k in (4, 2, 1) if blocks % k == 0)

    def find_active(step, found):
        members = [step * batch + k for k in range(batch)]
        tiles, points, limits = [], [], []
        for block in members:
            pieces = []
            for slot in range(slots):
                place = jnp.maximum(meta_ref[block, slot], 0)
                pieces.append(spheres[pl.ds(place * chunks, chunks), :])
            tiles.append(jnp.concatenate(pieces, axis=0))
            start = pl.multiple_of(block * LANES, LANES)
            points.append(moved_ref[:, pl.ds(start, LANES)])
        squares = [None] * batch
        for axis in range(3):
            centers = [jnp.broadcast_to(tile[:, axis : axis + 1], tile.shape) for tile in tiles]
            for k in range(batch):
                diff = centers[k] - points[k][axis : axis + 1]
                squares[k] = diff * diff if axis == 0 else squares[k] + diff * diff
        distances = [jnp.sqrt(square) for square in squares]
        close = [jnp.broadcast_to(tile[:, 4:5], tile.shape) for tile in tiles]
        radius = [jnp.broadcast_to(tile[:, 3:4], tile.shape) for tile in tiles]
        keeps = []
        for k, block in enumerate(members):
            real = dense_slot < meta_ref[block, slots]
            upper = jnp.where(real, distances[k] + close[k], big_value)
            upper = jnp.min(upper, axis=0, keepdims=True)
            flags = flags_ref[pl.ds(lax.axis_index("surf") * blocks + block, 1), :]
            limit = jnp.where(flags == 1, upper * 1.0001 + 1e-4, -big_value)
            keeps.append(jnp.where(real & (distances[k] - radius[k] <= limit), 1.0, 0.0))
        keeps = [jnp.max(keep, axis=1, keepdims=True) for keep in keeps]
        for k, block in enumerate(members):
            found = jnp.where(dense_lane == block, keeps[k], found)
        lefts_here = []
        for k in range(batch):
            half = jnp.concatenate([points[k], jnp.ones((1, LANES), jnp.float32)], axis=0)
            lefts_here.append(stack6(parts3(jnp.concatenate([half, half], axis=0)), LEFT))
        lefts_here = [jnp.transpose(left) for left in lefts_here]
        for k, block in enumerate(members):
            lefts[block] = lefts_here[k].astype(jnp.bfloat16)
            nearest[block] = jnp.full((LANES, LANES), big_value, jnp.float32)
        return found

    found = jnp.zeros((dense_rows, LANES), jnp.float32)
    active[...] = lax.fori_loop(0, blocks // batch, find_active, found).astype(jnp.int32)
    copy = pltpu.make_async_copy(active, active_scalars, sem)
    copy.start()
    copy.wait()

    shift = (blocks - 1).bit_length()
    scale = 1 << shift

    def list_block(block, items):
        def list_leaves(group, items):
            for k in range(LIST_SLOTS):
                slot = group * LIST_SLOTS + k
                place = jnp.maximum(meta_ref[block, jnp.minimum(slot, slots - 1)], 0)
                row = divide(place, leaf_dev) * (32 * rows - leaf_dev * chunks) + place * chunks
                code = (row << shift) + block
                for chunk in range(chunks):
                    work[items] = code + (chunk << shift)
                    items = items + active_scalars[slot * chunks + chunk, block]
            return items

        count = jnp.where(meta_ref[block, slots + 1] > 0, meta_ref[block, slots], 0)
        return lax.fori_loop(0, divide(count + LIST_SLOTS - 1, LIST_SLOTS), list_leaves, items)

    items = lax.fori_loop(0, blocks, list_block, 0)
    upper_rows = lax.broadcasted_iota(jnp.int32, (8, LANES), 0) < 4

    def split(code):
        return code & (scale - 1), lax.shift_right_logical(code, shift)

    def right_side(code):
        first = split(code)[1]
        tiles = []
        for pair in range((FUNCS + 1) // 2):
            parts = parts3(table[pl.ds(first + pair * 8 * rows, 8, stride=rows), :])
            for index in range(2):
                if pair * 2 + index < FUNCS:
                    mine = upper_rows if index == 0 else jnp.logical_not(upper_rows)
                    own = [jnp.where(mine, part, 0.0) for part in parts]
                    tiles.append(stack6(own, RIGHT))
        return jnp.concatenate(tiles, axis=1).astype(jnp.bfloat16)

    def products(block, right):
        return jnp.dot(lefts[block], right, preferred_element_type=jnp.float32)

    def evaluate(item, source):
        block, start = split(work[item])
        half_a, half_b, half_c = (
            jnp.broadcast_to(table[pl.ds(start + (28 + k) * rows, 1), :], (8, LANES)) for k in range(3)
        )
        for part in range(LANES // 8):
            here = slice(part * 8, part * 8 + 8)
            ta, sa, h, tb, sb, tc, sc = (
                source[here, k * LANES : (k + 1) * LANES] for k in range(FUNCS)
            )
            over_a = jnp.maximum(jnp.abs(ta) - half_a, 0.0)
            over_b = jnp.maximum(jnp.abs(tb) - half_b, 0.0)
            over_c = jnp.maximum(jnp.abs(tc) - half_c, 0.0)
            edge = jnp.minimum(sa * sa + over_a * over_a, sb * sb + over_b * over_b)
            edge = jnp.minimum(edge, sc * sc + over_c * over_c)
            inside = jnp.minimum(jnp.minimum(sa, sb), sc) >= 0.0
            square = jnp.where(inside, 0.0, edge) + h * h
            nearest[block, here] = jnp.minimum(nearest[block, here], square)

    @pl.when(items > 0)
    def _():
        for extra in range(3 * TOGETHER):
            work[items + extra] = work[items - 1]
        def product(code, right):
            return products(split(code)[0], right)

        for k in range(TOGETHER):
            products_of[k] = product(work[k], right_side(work[k]))
            rights[k] = right_side(work[TOGETHER + k])

        def some_items(step, carry):
            item = step * TOGETHER
            for k in range(TOGETHER):
                coming = product(work[item + TOGETHER + k], rights[k])
                evaluate(item + k, products_of.at[k])
                products_of[k] = coming
                rights[k] = right_side(work[item + 2 * TOGETHER + k])
            return carry

        lax.fori_loop(0, lax.div(items + TOGETHER - 1, TOGETHER), some_items, 0)

    def finish(block, carry):
        square = jnp.min(jnp.transpose(nearest[block]), axis=0, keepdims=True)
        flags = flags_ref[pl.ds(lax.axis_index("surf") * blocks + block, 1), :]
        wall_ref[pl.ds(block, 1), :] = jnp.where(flags == 1, jnp.sqrt(square), 0.0)
        return carry

    lax.fori_loop(0, blocks, finish, 0, unroll=2)


def vmem_params(scratch, operands):
    total = 0
    for ref in scratch:
        if getattr(ref, "memory_space", None) == pltpu.VMEM:
            rows, lanes = ref.shape[-2], ref.shape[-1]
            size = -(-rows // 16) * 16 * -(-lanes // LANES) * LANES * jnp.dtype(ref.dtype).itemsize
            for extent in ref.shape[:-2]:
                size *= extent
            total += size
    for operand in operands:
        total += 2 * operand.size * operand.dtype.itemsize
    return pltpu.CompilerParams(vmem_limit_bytes=min(total + 8 * 1024 * 1024, 60 * 1024 * 1024))


def gather_order(vol_count, surf_count):
    steps = []
    bit = surf_count // 2
    while bit >= 1:
        steps.append(("surf", bit))
        bit //= 2
    bit = vol_count // 2
    while bit >= 1:
        steps.append(("vol", bit))
        bit //= 2
    return steps


def body(surface_points, surface_shift, facet_nodes, volume_points, near_wall, candidates):
    surf_count, vol_count = lax.axis_size("surf"), lax.axis_size("vol")
    sizes = {"surf": surf_count, "vol": vol_count}
    leaf_dev, _, facet_len = facet_nodes.shape
    leaf_len = surface_points.shape[1] // leaf_dev
    halves, chunks = leaf_len // LANES, facet_len // LANES
    devices = surf_count * vol_count
    leaves = devices * leaf_dev
    slots = candidates.shape[1]
    blocks = candidates.shape[0] // surf_count
    share_len = volume_points.shape[1] // surf_count
    rows = leaf_dev * chunks
    payload_rows = leaf_dev * halves * 8 + 3 * rows
    vmem = pl.BlockSpec(memory_space=pltpu.VMEM)
    smem = pl.BlockSpec(memory_space=pltpu.SMEM)

    flag_rows = near_wall.reshape(-1, LANES)
    steps = gather_order(vol_count, surf_count)
    held, meta = pl.pallas_call(
        functools.partial(prep_kernel, steps, surf_count),
        out_shape=[
            jax.ShapeDtypeStruct((1, payload_rows, LANES), jnp.float32),
            jax.ShapeDtypeStruct((blocks, slots + 2), jnp.int32),
        ],
        in_specs=[vmem] * 5,
        out_specs=[vmem] * 2,
        scratch_shapes=[pltpu.VMEM(candidates.shape, jnp.int32)],
    )(surface_points, surface_shift, jnp.transpose(facet_nodes, (1, 0, 2)), flag_rows, jnp.transpose(candidates))
    for axis, bit in steps[:-1]:
        pairs = [(source, source ^ bit) for source in range(sizes[axis])]
        held = jnp.concatenate([held, lax.ppermute(held, axis, pairs)], axis=0)
    axis, bit = steps[-1]
    pairs = [(source, source ^ bit) for source in range(sizes[axis])]
    node_rows = leaf_dev * halves * 8
    held, held_ids = held[:, :node_rows], held[:, node_rows:]
    arrived = lax.ppermute(held, axis, pairs)
    arrived_ids = lax.ppermute(held_ids, axis, pairs)

    groups = -(-leaves // LANES)
    near_scratch = [
        pltpu.VMEM((leaves + 1, 8, leaf_len), jnp.float32),
        pltpu.VMEM((leaves + 1, 48, leaf_len), jnp.bfloat16),
        pltpu.VMEM((leaves + 1, 8, LANES), jnp.float32),
        pltpu.VMEM((8, groups * LANES), jnp.float32),
        pltpu.VMEM((blocks, 4, LANES, LANES), jnp.float32),
        pltpu.VMEM((NEAR_STEPS, NEAR_TOGETHER, LANES, leaf_len), jnp.float32),
        pltpu.VMEM((NEAR_STEPS, NEAR_TOGETHER, LANES, 48), jnp.bfloat16),
        pltpu.SMEM((blocks * (slots // NEAR_TOGETHER + 1) + 3 * NEAR_STEPS,), jnp.int32),
]
    disp, moved = pl.pallas_call(
        functools.partial(near_kernel, leaf_dev, halves),
        out_shape=[jax.ShapeDtypeStruct((3, share_len), jnp.float32)] * 2,
        in_specs=[smem, vmem, vmem, vmem],
        out_specs=[vmem, vmem],
        scratch_shapes=near_scratch,
        compiler_params=vmem_params(near_scratch, (held, arrived, volume_points)),
        cost_estimate=pl.CostEstimate(flops=10**10, bytes_accessed=10**6, transcendentals=10**6),
    )(meta, held, arrived, volume_points)
    wall_scratch = [
        pltpu.VMEM((devices * rows * 32, LANES), jnp.float32),
        pltpu.VMEM((devices * rows, LANES), jnp.float32),
        pltpu.VMEM((blocks, LANES, 48), jnp.bfloat16),
        pltpu.VMEM((blocks, LANES, LANES), jnp.float32),
        pltpu.VMEM((TOGETHER, 48, FUNCS * LANES), jnp.bfloat16),
        pltpu.VMEM((TOGETHER, LANES, FUNCS * LANES), jnp.float32),
        pltpu.VMEM((slots * chunks, LANES), jnp.int32),
        pltpu.SMEM((slots * chunks, LANES), jnp.int32),
        pltpu.SMEM((blocks * slots * chunks + 3 * TOGETHER,), jnp.int32),
        pltpu.SemaphoreType.DMA,
]
    wall = pl.pallas_call(
        functools.partial(wall_kernel, leaf_dev, halves, chunks),
        out_shape=jax.ShapeDtypeStruct((blocks, LANES), jnp.float32),
        in_specs=[smem] + [vmem] * 6,
        out_specs=vmem,
        scratch_shapes=wall_scratch,
        compiler_params=vmem_params(wall_scratch, (held, arrived, held_ids, arrived_ids, flag_rows, volume_points)),
    )(meta, held, arrived, held_ids, arrived_ids, moved, flag_rows)
    return (disp, wall.reshape(-1))


def solution(mesh):
    placed = (
        P(None, ("vol", "surf")),
        P(None, ("vol", "surf")),
        P(("vol", "surf"), None, None),
        P(None, "vol"),
        P("vol"),
        P("vol", None),
    )
    return jax.shard_map(
        body,
        mesh=mesh,
        in_specs=placed,
        out_specs=(P(None, ("vol", "surf")), P(("vol", "surf"))),
        check_vma=False,
    )
```
